32 devices in a mesh: dp: 2 (over y), expert: 16 (over z, x, core).
Axes of the slice: x: 2, y: 2, z: 4, core: 2. Of those that a mesh axis runs over, the one named last changes fastest.
Arguments:
- soft_tokens: bfloat16 [2048, 2048], P('expert', 'dp'), may hold values from -6 to 6
- expert_ids: int32 [2048, 8], P('expert'), may hold values from 0 to 31, all different within a row; in each aligned block of 128 rows (0 to 127, 128 to 255, ...) at most 40 rows name the same one
- gate_mix: float32 [2048, 8], P('expert'), may hold values from 0.05 to 0.35
- w_gate: bfloat16 [32, 2048, 768], P('expert', 'dp'), may hold values from -0.125 to 0.125
- w_up: bfloat16 [32, 2048, 768], P('expert', 'dp'), may hold values from -0.125 to 0.125
- w_down: bfloat16 [32, 768, 2048], P('expert', None, 'dp'), may hold values from -0.21875 to 0.21875
- out_grad: bfloat16 [2048, 2048], P('expert', 'dp'), may hold values from -6 to 6
Outputs:
- mixed: bfloat16 [2048, 2048], P('expert', 'dp')
- token_grad: bfloat16 [2048, 2048], P('expert', 'dp')
The draws below stay inside these ranges and needn't reach their ends.
Inputs may be any that keep to these rules, and one draw needn't show every extreme that they name: `expert_ids`: each row names 8 different experts. Among the 128 rows of one device no expert is named by more than 40 rows, and in some device one expert is named by exactly 40 rows.
All inputs are finite; a program needn't handle non-finite values.
Results may differ from the reference program's by a relative error of at most 0.023.
Values may be sent and summed in bfloat16 or wider, within the bound.
A program may use at most 128 MiB of HBM per device.

```python
import math
import jax
import jax.numpy as jnp
import numpy as np
from jax import lax

D = 2048
F = 768
TOPK = 8
TOK_DEV = 128
EXPERTS = 32
TOKENS = 2048
CAP = 40
N_DP = 2
N_EXPERT = 16


def block_scale(key, shape, pieces, least, high):
    def one(position, blocks):
        heights = jax.random.uniform(jax.random.fold_in(jax.random.fold_in(key, 6), position), (blocks,), jnp.float32, least / len(pieces), high / len(pieces))
        return jnp.repeat(jnp.exp(heights), shape[position] // blocks).reshape((-1,) + (1,) * (len(shape) - position - 1))

    gain = one(*pieces[0])
    for cut in pieces[1:]:
        gain = gain * one(*cut)
    return gain


def assign_block(stream_key, own, number, rows, count, top, most, slope):
    order = jax.random.permutation(stream_key, count)
    crowded, ordinary = load_shares(count, rows * top, most, slope, True), load_shares(count, rows * top, most, slope, False)
    places = jnp.arange(count)

    def named(lengths, offset_by):
        used = int((lengths > 0).sum())
        fixed = max(1, used // 4)
        passed = fixed + (places - fixed + offset_by * (used - fixed)) % max(1, count - fixed)
        return jnp.zeros((count,), jnp.int32).at[order[jnp.where(places < fixed, places, passed)]].set(jnp.asarray(lengths, jnp.int32))

    lengths = jnp.where(number % 4 == 0, named(crowded, number // 4), named(ordinary, number - number // 4 - 1))
    mixed = jax.random.permutation(jax.random.fold_in(own, 3), count)
    giver, sink = mixed[0:count // 2 * 2:2], mixed[1:count // 2 * 2:2]
    slack = jnp.minimum(lengths[giver] - 1, most - lengths[sink]) // 2
    slack = jnp.where((giver == order[0]) | (sink == order[0]) | (lengths[sink] == 0), 0, jnp.maximum(slack, 0))
    passed = jax.random.randint(jax.random.fold_in(own, 4), (count // 2,), 0, 1 << 20) % (slack + 1)
    lengths = lengths.at[giver].add(-passed).at[sink].add(passed)
    members = jnp.searchsorted(jnp.cumsum(lengths), jnp.arange(rows * top), side="right").astype(jnp.int32)
    table = members.reshape(top, rows).T
    table = table[jax.random.permutation(jax.random.fold_in(own, 1), rows)]
    offset_by = jax.random.randint(jax.random.fold_in(own, 2), (rows, 1), 0, top)
    return jnp.take_along_axis(table, (jnp.arange(top)[None, :] + offset_by) % top, axis=1)


def load_shares(count, total, limit, lean, full):
    loads = [(1 << 20) // math.isqrt(rank ** lean) + 1 for rank in range(1, count + 1)]
    largest = limit if full else min(limit, max(-(-total // count), total * loads[0] // sum(loads)))
    least = 1 if total - largest >= count - 1 else 0
    holding, surplus = [largest] + [least] * (count - 1), total - largest - least * (count - 1)
    while surplus > 0:
        free = [i for i in range(1, count) if holding[i] < largest] or [i for i in range(1, count) if holding[i] < limit]
        whole, remaining = sum([loads[i] for i in free]), surplus
        for i in free:
            addition = min(limit - holding[i], max(1, remaining * loads[i] // whole), surplus)
            holding[i] = holding[i] + addition
            surplus = surplus - addition
    return np.array(holding)


def scatter_about(stream_key, shape, spread, reach, shards=(), held_as=jnp.bfloat16):
    entries = spread * jax.random.normal(stream_key, shape, jnp.float32)
    if shards:
        entries = entries * block_scale(stream_key, shape, shards, -0.22, 0.18)
    return jnp.clip(entries, -reach, reach).astype(held_as)


def setup_inputs(seed: int = 0) -> dict:
    seeds = jax.random.split(jax.random.key(seed), 8)
    soft_tokens = scatter_about(seeds[0], (TOKENS, D), 1.0, 6.0, ((0, 16), (1, 2)))
    expert_ids_keys = jax.random.split(jax.random.fold_in(seeds[1], 1), TOKENS // TOK_DEV)
    expert_ids_turns = jax.random.permutation(jax.random.fold_in(seeds[1], 3), TOKENS // TOK_DEV)
    expert_ids = jax.vmap(lambda own, number: assign_block(jax.random.fold_in(seeds[1], 2), own, number, TOK_DEV, EXPERTS, TOPK, CAP, 2))(expert_ids_keys, expert_ids_turns).reshape((TOKENS, TOPK))
    gate_mix = jnp.clip(0.05 + 0.29999999 * jax.random.uniform(seeds[2], (TOKENS, TOPK), jnp.float32) ** block_scale(seeds[2], (TOKENS, TOPK), ((0, 16),), -0.2, 0.2), 0.05, 0.35)
    w_gate = scatter_about(seeds[3], (EXPERTS, D, F), D ** -0.5, 0.125, ((0, 16), (1, 2)))
    w_up = scatter_about(seeds[4], (EXPERTS, D, F), D ** -0.5, 0.125, ((0, 16), (1, 2)))
    w_down = scatter_about(seeds[5], (EXPERTS, F, D), F ** -0.5, 0.21875, ((0, 16), (2, 2)))
    out_grad = scatter_about(seeds[6], (TOKENS, D), 1.0, 6.0, ((0, 16), (1, 2)))
    return dict(soft_tokens=soft_tokens, expert_ids=expert_ids, gate_mix=gate_mix, w_gate=w_gate, w_up=w_up, w_down=w_down, out_grad=out_grad)


def activate(sums, hidden):
    gate_part = sums[:, :hidden]
    upper_part = sums[:, hidden:]
    sigmoid_gate = jax.nn.sigmoid(gate_part)
    return (gate_part * sigmoid_gate * upper_part).astype(jnp.bfloat16)

def act_grad(sums, back, hidden):
    gate_part = sums[:, :hidden]
    upper_part = sums[:, hidden:]
    sigmoid_gate = jax.nn.sigmoid(gate_part)
    d_gate = back * upper_part * sigmoid_gate * (1.0 + gate_part * (1.0 - sigmoid_gate))
    d_upper = back * gate_part * sigmoid_gate
    return jnp.concatenate([d_gate, d_upper], axis=1).astype(jnp.bfloat16)

def block_sum(rows, weight):
    width_part = D // N_DP
    total = jnp.zeros((rows.shape[0], weight.shape[1]), jnp.float32)
    for part in range(N_DP):
        term = jnp.dot(rows[:, part * width_part:(part + 1) * width_part], weight[part * width_part:(part + 1) * width_part], preferred_element_type=jnp.float32).astype(jnp.bfloat16)
        total = total + lax.optimization_barrier(term).astype(jnp.float32)
    return total

def reference(soft_tokens, expert_ids, gate_mix, w_gate, w_up, w_down, out_grad):
    flat_count = TOKENS * TOPK
    slots = N_EXPERT * CAP
    block_ids = expert_ids.reshape(N_EXPERT, TOK_DEV * TOPK)
    onehot = (block_ids[:, :, None] == jnp.arange(EXPERTS, dtype=jnp.int32)[None, None, :]).astype(jnp.int32)
    before = lax.optimization_barrier(jnp.sum(jnp.cumsum(onehot, axis=1) * onehot, axis=2)) - 1
    column = jnp.arange(N_EXPERT, dtype=jnp.int32)[:, None] * CAP + before
    table = jnp.full((EXPERTS, slots), flat_count, jnp.int32)
    table = table.at[block_ids, column].set(jnp.arange(flat_count, dtype=jnp.int32).reshape(N_EXPERT, TOK_DEV * TOPK))
    w_both = jnp.concatenate([w_gate, w_up], axis=2)
    flat_mix = gate_mix.reshape(flat_count)

    def one_expert(carry, index):
        mixed, grad_in = carry
        entry = table[index]
        valid = entry < flat_count
        token = jnp.minimum(entry // TOPK, TOKENS - 1).astype(jnp.int32)
        weight = jnp.where(valid, flat_mix[jnp.minimum(entry, flat_count - 1)], 0.0)
        rows = jnp.where(valid[:, None], soft_tokens[token], jnp.zeros((), soft_tokens.dtype))
        grads = jnp.where(valid[:, None], out_grad[token], jnp.zeros((), out_grad.dtype))
        both = w_both[index]
        down = w_down[index]
        sums = block_sum(rows, both)
        hidden = activate(sums, F)
        expert_out = jnp.dot(hidden, down, preferred_element_type=jnp.float32).astype(jnp.bfloat16)
        back = block_sum(grads, down.T)
        dpre = act_grad(sums, back, F)
        grad_rows = jnp.dot(dpre, both.T, preferred_element_type=jnp.float32).astype(jnp.bfloat16)
        mixed = mixed.at[token].add(weight[:, None] * expert_out.astype(jnp.float32))
        grad_in = grad_in.at[token].add(weight[:, None] * grad_rows.astype(jnp.float32))
        return ((mixed, grad_in), None)
    start = (jnp.zeros((TOKENS, D), jnp.float32), jnp.zeros((TOKENS, D), jnp.float32))
    (mixed, grad_in), unused = lax.scan(one_expert, start, jnp.arange(EXPERTS, dtype=jnp.int32))
    return (mixed.astype(jnp.bfloat16), grad_in.astype(jnp.bfloat16))
```

```python
import functools

import jax
import jax.numpy as jnp
from jax import lax
from jax.experimental import pallas as pl
from jax.experimental.pallas import tpu as pltpu
from jax.sharding import PartitionSpec as P

F32 = jnp.float32
BF16 = jnp.bfloat16


def slot_maps(ids, mix, first, local_experts, capacity):
    tok_rows = ids.shape[1]
    own = first + jnp.arange(local_experts, dtype=jnp.int32)
    hit = ids[:, None, :, :] == own[None, :, None, None]
    named = jnp.any(hit, axis=3)
    weight = jnp.sum(jnp.where(hit, mix[:, None, :, :], 0.0), axis=3)
    before = jnp.arange(tok_rows)[:, None] < jnp.arange(tok_rows)[None, :]
    place = jnp.einsum(
        "set,tu->seu", named.astype(BF16), before.astype(BF16), preferred_element_type=F32
    ).astype(jnp.int32)
    slots = jnp.arange(capacity, dtype=jnp.int32)
    pick = (place[:, :, None, :] == slots[None, None, :, None]) & named[:, :, None, :]
    slot_weight = jnp.sum(jnp.where(pick, weight[:, :, None, :], 0.0), axis=3)
    return pick.astype(BF16), slot_weight


def per_device(soft_tokens, expert_ids, gate_mix, w_gate, w_up, w_down, out_grad):
    tok_rows, width_part = soft_tokens.shape
    top_count = expert_ids.shape[1]
    local_experts = w_gate.shape[0]
    hidden = w_gate.shape[2]
    groups = lax.axis_size("expert")
    dp_count = lax.axis_size("dp")
    experts = groups * local_experts
    capacity = max(2, tok_rows * top_count * 5 // (4 * experts))
    both = lax.all_gather(jnp.concatenate([soft_tokens, out_grad], axis=1), "expert")
    ids = lax.all_gather(expert_ids, "expert")
    mix = lax.all_gather(gate_mix, "expert")
    first = lax.axis_index("expert") * local_experts
    pick, slot_weight = slot_maps(ids, mix, first, local_experts, capacity)
    rows = jnp.einsum("sect,std->secd", pick, both, preferred_element_type=F32).astype(BF16)
    pre = [
        jnp.einsum("secd,edf->secf", rows[..., :width_part], w, preferred_element_type=F32)
        for w in (w_gate, w_up)
    ]
    back = jnp.einsum("secd,efd->secf", rows[..., width_part:], w_down, preferred_element_type=F32)
    part = jnp.concatenate(pre + [back], axis=-1).astype(BF16)
    total = part.astype(F32)
    moved = part
    for _ in range(dp_count - 1):
        moved = lax.ppermute(moved, "dp", [(i, (i + 1) % dp_count) for i in range(dp_count)])
        total = total + moved.astype(F32)
    a = total[..., :hidden]
    b = total[..., hidden : 2 * hidden]
    back = total[..., 2 * hidden :] * slot_weight[..., None]
    sig = jax.nn.sigmoid(a)
    act = (a * sig * b * slot_weight[..., None]).astype(BF16)
    d_gate = (back * b * sig * (1.0 + a * (1.0 - sig))).astype(BF16)
    d_up = (back * a * sig).astype(BF16)
    out = jnp.einsum("secf,efd->secd", act, w_down, preferred_element_type=F32)
    grad = jnp.einsum("secf,edf->secd", d_gate, w_gate, preferred_element_type=F32) + jnp.einsum(
        "secf,edf->secd", d_up, w_up, preferred_element_type=F32
    )
    result = jnp.concatenate([out, grad], axis=-1).astype(BF16)
    spread = jnp.einsum("sect,secd->std", pick, result, preferred_element_type=F32).astype(BF16)
    summed = lax.psum_scatter(spread, "expert", scatter_dimension=0, tiled=False)
    return summed[:, :width_part], summed[:, width_part:]


MESH = pl.DeviceIdType.MESH
MID = 2
CORES = 2
AHEAD = 2


def flip(value, step, count):
    out, bit = 0, 1
    while bit < count:
        out = out + lax.rem(lax.div(value, bit) + lax.div(step, bit), 2) * bit
        bit *= 2
    return out


def fused_kernel(
    groups, slots, tok_ref, cot_ref, ids_ref, mix_ref, wg_hbm, wu_hbm, wd_hbm, mixed_ref, tgrad_ref,
    wg_ref, wu_ref, wd_ref, ag_tok, ag_cot, table, metas,
    ysend_pre, yrecv_pre, ysend_back, yrecv_back, acc, crecv, hold, xsend, xrecv, zsend, zrecv,
    wsem, ms, mr, zs, zr, xs, xr, cs, cr, ys, yr, rcs, rcr, rxs, rxr, rzs, rzr,
):
    rows, half = tok_ref.shape
    experts, _, hid = wg_ref.shape
    plane = MID * CORES
    outer = groups // plane
    units = 2 * outer
    me = lax.axis_index("expert")
    y = lax.axis_index("dp")
    z = lax.div(me, plane)
    x = lax.rem(lax.div(me, CORES), MID)
    c = lax.rem(me, CORES)
    core_peer = (z * MID + x) * CORES + 1 - c
    x_peer = (z * MID + 1 - x) * CORES + c
    other_dp = {"dp": 1 - y, "expert": me}
    ag = (ag_tok, ag_cot)
    own = (tok_ref, cot_ref)
    ysend, yrecv = (ysend_pre, ysend_back), (yrecv_pre, yrecv_back)

    def at(expert):
        return {"dp": y, "expert": expert}

    def copy(src, dst, send, recv, device):
        return pltpu.make_async_remote_copy(
            src_ref=src, dst_ref=dst, send_sem=send, recv_sem=recv,
            device_id=device, device_id_type=MESH,
        )

    barrier = pltpu.get_barrier_semaphore()
    for k in range(1, groups):
        pl.semaphore_signal(
            barrier, inc=1, device_id=at(lax.rem(me + k, groups)), device_id_type=MESH
        )
    pl.semaphore_signal(barrier, inc=1, device_id=other_dp, device_id_type=MESH)

    loads = [
        pltpu.make_async_copy(src, dst, wsem.at[k])
        for k, (src, dst) in enumerate(((wg_hbm, wg_ref), (wu_hbm, wu_ref), (wd_hbm, wd_ref)))
    ]
    for load in loads:
        load.start()

    def dot(a, b, dims):
        return lax.dot_general(a, b, (dims, ((), ())), preferred_element_type=F32)

    def make_table():
        total = groups * experts
        expert = lax.broadcasted_iota(jnp.int32, (total, rows), 0)
        named = jnp.zeros((total, rows), F32)
        weight = jnp.zeros((total, rows), F32)
        for k in range(ids_ref.shape[0]):
            hit = expert == ids_ref[k : k + 1, :]
            named = named + jnp.where(hit, 1.0, 0.0)
            weight = weight + jnp.where(hit, mix_ref[k : k + 1, :], 0.0)
        before = lax.broadcasted_iota(jnp.int32, (rows, rows), 0) < lax.broadcasted_iota(
            jnp.int32, (rows, rows), 1
        )
        before = jnp.where(before, 1.0, 0.0).astype(BF16)
        place = dot(named.astype(BF16), before, ((1,), (0,)))
        key = jnp.where(named > 0.0, place, -4.0 * slots)
        table[...] = jnp.zeros_like(table)
        for d in range(groups):
            span = slice(d * experts, (d + 1) * experts)
            table[d, :experts, :] = key[span]
            table[d, experts : 2 * experts, :] = weight[span]

    make_table()
    ag_tok[me] = tok_ref[...]
    ag_cot[me] = cot_ref[...]
    metas[me] = table[me]
    pl.semaphore_wait(barrier, groups)

    def meta_copy(to):
        return copy(table.at[to], metas.at[me], ms.at[to], mr.at[me], at(to))

    def meta_arrival(source):
        return copy(table.at[source], metas.at[source], ms.at[source], mr.at[source], at(source))

    def peer_of(step):
        return (flip(z, step, outer) * MID + x) * CORES + c

    def z_copy(step, part):
        return copy(own[part], ag[part].at[me], zs.at[step, part], zr.at[step, part], at(peer_of(step)))

    def z_arrival(step, part):
        blk = peer_of(step)
        return copy(own[part], ag[part].at[blk], zs.at[step, part], zr.at[step, part], at(blk))

    def x_copy(step, part, blk):
        return copy(
            ag[part].at[blk], ag[part].at[blk], xs.at[step, part], xr.at[step, part], at(x_peer)
        )

    def c_copy(step, across, part, blk):
        return copy(
            ag[part].at[blk], ag[part].at[blk],
            cs.at[step, across, part], cr.at[step, across, part], at(core_peer),
        )

    def y_copy(u, part):
        return copy(ysend[part].at[u], yrecv[part].at[u], ys.at[u, part], yr.at[u, part], other_dp)

    def rc_copy(u, part):
        return copy(
            acc.at[part, 1 - c], crecv.at[u, part], rcs.at[u, part], rcr.at[u, part], at(core_peer)
        )

    def rx_copy(step, part):
        return copy(
            xsend.at[step, part], xrecv.at[step, part],
            rxs.at[step, part], rxr.at[step, part], at(x_peer),
        )

    def rz_copy(step, part):
        return copy(
            zsend.at[step, part], zrecv.at[step, part],
            rzs.at[step, part], rzr.at[step, part], at(peer_of(step)),
        )

    def step_of(u):
        g = lax.rem(lax.div(u + 1, 2), outer)
        return (lax.rem(g, outer - 1) + 1) * lax.div(g + outer - 1, outer)

    def across_of(u):
        first = 1 - lax.div(u + units - 1, units)
        last = lax.div(u + 1, units)
        return lax.rem(u + 1, 2) + last - first

    def base_of(u):
        across = across_of(u)
        return (flip(z, step_of(u), outer) * MID + x + across - 2 * x * across) * CORES

    order = [step for step in range(2, outer)] + [1]

    for part in range(2):
        c_copy(0, 0, part, me).start()
    meta_copy(core_peer).start()
    for part in range(2):
        z_copy(order[0], part).start()
    for part in range(2):
        x_copy(0, part, me).start()

    @pl.loop(1, groups)
    def _(k):
        to = lax.rem(me + k, groups)

        @pl.when(to != core_peer)
        def _():
            meta_copy(to).start()

    for part in range(2):
        for step in order[-1:] if outer > 2 else []:
            z_copy(step, part).start()

    def pick_of(u):
        base = base_of(u)
        tiles = metas[pl.ds(base, CORES)]
        slot = lax.broadcasted_iota(jnp.int32, (CORES * slots, CORES * rows), 0).astype(F32)
        picks, weights = [], []
        for e in range(experts):
            line = jnp.concatenate(
                [tiles[b, e : e + 1] + float(b * slots) for b in range(CORES)], axis=1
            )
            share = jnp.concatenate(
                [tiles[b, experts + e : experts + e + 1] for b in range(CORES)], axis=1
            )
            match = slot == line
            picks.append(jnp.where(match, 1.0, 0.0))
            weights.append(jnp.sum(jnp.where(match, share, 0.0), axis=1, keepdims=True))
        return jnp.concatenate(picks, axis=0), weights

    lines = CORES * slots

    def first_half(u):
        step, across, base = step_of(u), across_of(u), base_of(u)
        col = base + c

        def arrive(part):
            @pl.when(across > 0)
            def _():
                x_copy(step, part, col).wait_recv()
                c_copy(step, 1, part, col).start()

            @pl.when((1 - across) * step > 0)
            def _():
                z_arrival(step, part).wait_recv()
                x_copy(step, part, col).start()
                c_copy(step, 0, part, col).start()

            c_copy(step, across, part, base + 1 - c).wait_recv()

        arrive(0)

        @pl.when(u == 0)
        def _():
            meta_arrival(core_peer).wait_recv()

        @pl.when(u == 1)
        def _():
            @pl.loop(1, groups)
            def _(k):
                source = lax.rem(me + k, groups)

                @pl.when(source != core_peer)
                def _():
                    meta_arrival(source).wait_recv()

        pick, _ = pick_of(u)
        pick = pick.astype(BF16)

        def rows_of(part):
            block = ag[part][pl.ds(base, CORES)].reshape(CORES * rows, half)
            return dot(pick, block, ((1,), (0,))).astype(BF16)

        got = rows_of(0)

        @pl.when(u == 0)
        def _():
            loads[0].wait()
            loads[1].wait()

        for e in range(experts):
            mine = got[e * lines : (e + 1) * lines]
            ysend_pre[u, e, :, :hid] = dot(mine, wg_ref[e], ((1,), (0,))).astype(BF16)
            ysend_pre[u, e, :, hid:] = dot(mine, wu_ref[e], ((1,), (0,))).astype(BF16)
        y_copy(u, 0).start()
        arrive(1)
        got = rows_of(1)

        @pl.when(u == 0)
        def _():
            loads[2].wait()

        for e in range(experts):
            mine = got[e * lines : (e + 1) * lines]
            ysend_back[u, e] = dot(mine, wd_ref[e], ((1,), (1,))).astype(BF16)

        @pl.when(u > 0)
        def _():
            y_copy(u, 1).start()

        @pl.when(u == units - 1)
        def _():
            y_copy(0, 1).start()

        for i, step_now in enumerate(order[1:-1]):
            @pl.when(u == 2 * i + 1)
            def _():
                for part in range(2):
                    z_copy(step_now, part).start()

    def sums(u, e):
        def total(lo):
            piece = ysend_pre[u, e, :, lo : lo + hid].astype(F32)
            return piece + yrecv_pre[u, e, :, lo : lo + hid].astype(F32)

        return total(0), total(hid)

    def scatter(u, part, pick, values):
        spread = dot(pick.T.astype(BF16), jnp.concatenate(values, axis=0), ((1,), (0,)))
        acc[part] = spread.astype(BF16).reshape(CORES, rows, half)
        rc_copy(u, part).start()

    def mixed_half(u):
        pick, weights = pick_of(u)
        y_copy(u, 0).wait_recv()
        outs = []
        for e in range(experts):
            a, b = sums(u, e)
            act = (a * jax.nn.sigmoid(a) * b * weights[e]).astype(BF16)
            outs.append(dot(act, wd_ref[e], ((1,), (0,))).astype(BF16))
        scatter(u, 0, pick, outs)

    def grad_half(u):
        pick, weights = pick_of(u)
        y_copy(u, 1).wait_recv()
        grads = []
        for e in range(experts):
            a, b = sums(u, e)
            back = ysend_back[u, e].astype(F32) + yrecv_back[u, e].astype(F32)
            back = back * weights[e]
            sig = jax.nn.sigmoid(a)
            d_gate = (back * b * sig * (1.0 + a * (1.0 - sig))).astype(BF16)
            d_up = (back * a * sig).astype(BF16)
            grads.append(
                (dot(d_gate, wg_ref[e], ((1,), (1,))) + dot(d_up, wu_ref[e], ((1,), (1,)))).astype(BF16)
            )
        scatter(u, 1, pick, grads)

    def to_x_peer(u, part):
        step, across = step_of(u), across_of(u)
        rc_copy(u, part).wait_recv()
        both = (acc[part, c].astype(F32) + crecv[u, part].astype(F32)).astype(BF16)

        @pl.when(across == 0)
        def _():
            hold[step, part] = both

        @pl.when(across > 0)
        def _():
            xsend[step, part] = both
            rx_copy(step, part).start()

        rc_copy(u, part).wait_send()

    def to_owner(step, part):
        rx_copy(step, part).wait_recv()
        here = hold[step, part].astype(F32) + xrecv[step, part].astype(F32)
        zsend[step, part] = here.astype(BF16)
        rz_copy(step, part).start()

    @pl.loop(0, units + AHEAD)
    def _(i):
        @pl.when(i < units)
        def _():
            first_half(i)

        @pl.when(i >= AHEAD)
        def _():
            u = i - AHEAD

            @pl.when((u > 1) & (lax.rem(u, 2) == 1))
            def _():
                for part in range(2):
                    to_owner(step_of(u - 1), part)

            mixed_half(u)
            to_x_peer(u, 0)

            @pl.when(u > 0)
            def _():
                grad_half(u)
                to_x_peer(u, 1)

    def finish(part, out_ref):
        rx_copy(0, part).wait_recv()
        final = hold[0, part].astype(F32) + xrecv[0, part].astype(F32)
        for step in order:
            rz_copy(step, part).wait_recv()
            final = final + zrecv[step, part].astype(F32)
        out_ref[...] = final.astype(BF16)

    finish(0, mixed_ref)
    grad_half(0)
    to_x_peer(0, 1)
    finish(1, tgrad_ref)

    @pl.loop(1, groups)
    def _(k):
        meta_copy(lax.rem(me + k, groups)).wait_send()

    for part in range(2):
        for step in range(outer):
            x_copy(step, part, me).wait_send()
            rx_copy(step, part).wait_send()
            for across in range(2):
                c_copy(step, across, part, me).wait_send()
            if step:
                z_copy(step, part).wait_send()
                rz_copy(step, part).wait_send()
        for u in range(units):
            y_copy(u, part).wait_send()


def fused_device(soft_tokens, expert_ids, gate_mix, w_gate, w_up, w_down, out_grad):
    tok_rows, width_part = soft_tokens.shape
    top_count = expert_ids.shape[1]
    local_experts, _, hid = w_gate.shape
    groups = lax.axis_size("expert")
    experts = groups * local_experts
    capacity = max(2, tok_rows * top_count * 5 // (4 * experts))
    plane = MID * CORES
    outer = groups // plane
    units = 2 * outer
    lines = CORES * capacity
    vmem = pl.BlockSpec(memory_space=pltpu.VMEM)
    hbm = pl.BlockSpec(memory_space=pl.ANY)
    dma = pltpu.SemaphoreType.DMA
    out = jax.ShapeDtypeStruct((tok_rows, width_part), BF16)
    table_rows = -(-2 * local_experts // 8) * 8
    block = (tok_rows, width_part)
    return pl.pallas_call(
        functools.partial(fused_kernel, groups, capacity),
        out_shape=(out, out),
        in_specs=[vmem] * 4 + [hbm] * 3,
        out_specs=(vmem, vmem),
        scratch_shapes=[
            pltpu.VMEM(w_gate.shape, BF16),
            pltpu.VMEM(w_up.shape, BF16),
            pltpu.VMEM(w_down.shape, BF16),
            pltpu.VMEM((groups, *block), BF16),
            pltpu.VMEM((groups, *block), BF16),
            pltpu.VMEM((groups, table_rows, tok_rows), F32),
            pltpu.VMEM((groups, table_rows, tok_rows), F32),
            pltpu.VMEM((units, local_experts, lines, 2 * hid), BF16),
            pltpu.VMEM((units, local_experts, lines, 2 * hid), BF16),
            pltpu.VMEM((units, local_experts, lines, hid), BF16),
            pltpu.VMEM((units, local_experts, lines, hid), BF16),
            pltpu.VMEM((2, CORES, *block), BF16),
            pltpu.VMEM((units, 2, *block), BF16),
            pltpu.VMEM((outer, 2, *block), BF16),
            pltpu.VMEM((outer, 2, *block), BF16),
            pltpu.VMEM((outer, 2, *block), BF16),
            pltpu.VMEM((outer, 2, *block), BF16),
            pltpu.VMEM((outer, 2, *block), BF16),
            dma((3,)),
            dma((groups,)), dma((groups,)),
            dma((outer, 2)), dma((outer, 2)),
            dma((outer, 2)), dma((outer, 2)),
            dma((outer, 2, 2)), dma((outer, 2, 2)),
            dma((units, 2)), dma((units, 2)),
            dma((units, 2)), dma((units, 2)),
            dma((outer, 2)), dma((outer, 2)),
            dma((outer, 2)), dma((outer, 2)),
        ],
        compiler_params=pltpu.CompilerParams(
            collective_id=0, has_side_effects=True, vmem_limit_bytes=67043328
        ),
    )(soft_tokens, out_grad, expert_ids.T, gate_mix.T, w_gate, w_up, w_down)


def solution(mesh):
    in_specs = (
        P("expert", "dp"),
        P("expert", None),
        P("expert", None),
        P("expert", "dp", None),
        P("expert", "dp", None),
        P("expert", None, "dp"),
        P("expert", "dp"),
    )
    out_specs = (P("expert", "dp"), P("expert", "dp"))
    fits = mesh.shape["dp"] == 2 and mesh.shape["expert"] in (8, 16)
    return jax.shard_map(
        fused_device if fits else per_device,
        mesh=mesh, in_specs=in_specs, out_specs=out_specs, check_vma=False,
    )
```

```python
import functools

import jax
import jax.numpy as jnp
from jax import lax
from jax.experimental import pallas as pl
from jax.experimental.pallas import tpu as pltpu
from jax.sharding import PartitionSpec as P

F32 = jnp.float32
BF16 = jnp.bfloat16


def slot_maps(ids, mix, first, local_experts, capacity):
    tok_rows = ids.shape[1]
    own = first + jnp.arange(local_experts, dtype=jnp.int32)
    hit = ids[:, None, :, :] == own[None, :, None, None]
    named = jnp.any(hit, axis=3)
    weight = jnp.sum(jnp.where(hit, mix[:, None, :, :], 0.0), axis=3)
    before = jnp.arange(tok_rows)[:, None] < jnp.arange(tok_rows)[None, :]
    place = jnp.einsum(
        "set,tu->seu", named.astype(BF16), before.astype(BF16), preferred_element_type=F32
    ).astype(jnp.int32)
    slots = jnp.arange(capacity, dtype=jnp.int32)
    pick = (place[:, :, None, :] == slots[None, None, :, None]) & named[:, :, None, :]
    slot_weight = jnp.sum(jnp.where(pick, weight[:, :, None, :], 0.0), axis=3)
    return pick.astype(BF16), slot_weight


def per_device(soft_tokens, expert_ids, gate_mix, w_gate, w_up, w_down, out_grad):
    tok_rows, width_part = soft_tokens.shape
    top_count = expert_ids.shape[1]
    local_experts = w_gate.shape[0]
    hidden = w_gate.shape[2]
    groups = lax.axis_size("expert")
    dp_count = lax.axis_size("dp")
    experts = groups * local_experts
    capacity = max(2, tok_rows * top_count * 5 // (4 * experts))
    both = lax.all_gather(jnp.concatenate([soft_tokens, out_grad], axis=1), "expert")
    ids = lax.all_gather(expert_ids, "expert")
    mix = lax.all_gather(gate_mix, "expert")
    first = lax.axis_index("expert") * local_experts
    pick, slot_weight = slot_maps(ids, mix, first, local_experts, capacity)
    rows = jnp.einsum("sect,std->secd", pick, both, preferred_element_type=F32).astype(BF16)
    pre = [
        jnp.einsum("secd,edf->secf", rows[..., :width_part], w, preferred_element_type=F32)
        for w in (w_gate, w_up)
    ]
    back = jnp.einsum("secd,efd->secf", rows[..., width_part:], w_down, preferred_element_type=F32)
    part = jnp.concatenate(pre + [back], axis=-1).astype(BF16)
    total = part.astype(F32)
    moved = part
    for _ in range(dp_count - 1):
        moved = lax.ppermute(moved, "dp", [(i, (i + 1) % dp_count) for i in range(dp_count)])
        total = total + moved.astype(F32)
    a = total[..., :hidden]
    b = total[..., hidden : 2 * hidden]
    back = total[..., 2 * hidden :] * slot_weight[..., None]
    sig = jax.nn.sigmoid(a)
    act = (a * sig * b * slot_weight[..., None]).astype(BF16)
    d_gate = (back * b * sig * (1.0 + a * (1.0 - sig))).astype(BF16)
    d_up = (back * a * sig).astype(BF16)
    out = jnp.einsum("secf,efd->secd", act, w_down, preferred_element_type=F32)
    grad = jnp.einsum("secf,edf->secd", d_gate, w_gate, preferred_element_type=F32) + jnp.einsum(
        "secf,edf->secd", d_up, w_up, preferred_element_type=F32
    )
    result = jnp.concatenate([out, grad], axis=-1).astype(BF16)
    spread = jnp.einsum("sect,secd->std", pick, result, preferred_element_type=F32).astype(BF16)
    summed = lax.psum_scatter(spread, "expert", scatter_dimension=0, tiled=False)
    return summed[:, :width_part], summed[:, width_part:]


MESH = pl.DeviceIdType.MESH
MID = 2
CORES = 2
AHEAD = 4


def same(a, b):
    gap = (a - b) * (a - b)
    return 1 - lax.div(2 * gap, gap + 1)


def flip(value, step, count):
    out, bit = 0, 1
    while bit < count:
        out = out + lax.rem(lax.div(value, bit) + lax.div(step, bit), 2) * bit
        bit *= 2
    return out


def fused_kernel(
    groups, slots, tok_hbm, cot_hbm, ids_hbm, mix_hbm, wg_hbm, wu_hbm, wd_hbm, mixed_hbm, tgrad_hbm,
    ids_ref, mix_ref, wg_ref, wu_ref, wd_ref, ag_tok, ag_cot, table, metas,
    ysend_pre, yrecv_pre, ysend_back, yrecv_back, ready, acc, crecv, hold, xsend, xrecv, zsend, zrecv,
    lsem, wsem, osem, ms, mr, zs, zr, xs, xr, cs, cr, ys, yr, rcs, rcr, rxs, rxr, rzs, rzr,
):
    rows, half = tok_hbm.shape
    experts, _, hid = wg_ref.shape
    plane = MID * CORES
    outer = groups // plane
    units = 2 * outer
    me = lax.axis_index("expert")
    y = lax.axis_index("dp")
    z = lax.div(me, plane)
    x = lax.rem(lax.div(me, CORES), MID)
    c = lax.rem(me, CORES)
    core_peer = (z * MID + x) * CORES + 1 - c
    x_peer = (z * MID + 1 - x) * CORES + c
    other_dp = {"dp": 1 - y, "expert": me}
    ag = (ag_tok, ag_cot)
    outputs = (mixed_hbm, tgrad_hbm)
    ysend, yrecv = (ysend_pre, ysend_back), (yrecv_pre, yrecv_back)

    def at(expert):
        return {"dp": y, "expert": expert}

    def copy(src, dst, send, recv, device):
        return pltpu.make_async_remote_copy(
            src_ref=src, dst_ref=dst, send_sem=send, recv_sem=recv,
            device_id=device, device_id_type=MESH,
        )

    barrier = pltpu.get_barrier_semaphore()
    for k in range(1, groups):
        pl.semaphore_signal(
            barrier, inc=1, device_id=at(lax.rem(me + k, groups)), device_id_type=MESH
        )
    pl.semaphore_signal(barrier, inc=1, device_id=other_dp, device_id_type=MESH)

    loads = [
        pltpu.make_async_copy(src, dst, lsem.at[k])
        for k, (src, dst) in enumerate(
            ((ids_hbm, ids_ref), (mix_hbm, mix_ref), (tok_hbm, ag_tok.at[me]), (cot_hbm, ag_cot.at[me]))
        )
    ]

    def weight(which, e):
        src, dst = ((wg_hbm, wg_ref), (wu_hbm, wu_ref), (wd_hbm, wd_ref))[which]
        return pltpu.make_async_copy(src.at[e], dst.at[e], wsem.at[which, e])

    for load in loads:
        load.start()
    for e in range(experts):
        for which in range(3):
            weight(which, e).start()

    def dot(a, b, dims):
        return lax.dot_general(a, b, (dims, ((), ())), preferred_element_type=F32)

    def make_table():
        total = groups * experts
        expert = lax.broadcasted_iota(jnp.int32, (total, rows), 0)
        named = jnp.zeros((total, rows), F32)
        weight = jnp.zeros((total, rows), F32)
        for k in range(ids_ref.shape[0]):
            hit = expert == ids_ref[k : k + 1, :]
            named = named + jnp.where(hit, 1.0, 0.0)
            weight = weight + jnp.where(hit, mix_ref[k : k + 1, :], 0.0)
        before = lax.broadcasted_iota(jnp.int32, (rows, rows), 0) < lax.broadcasted_iota(
            jnp.int32, (rows, rows), 1
        )
        before = jnp.where(before, 1.0, 0.0).astype(BF16)
        place = dot(named.astype(BF16), before, ((1,), (0,)))
        key = jnp.where(named > 0.0, place, -4.0 * slots)
        table[...] = jnp.zeros_like(table)
        for d in range(groups):
            span = slice(d * experts, (d + 1) * experts)
            table[d, :experts, :] = key[span]
            table[d, experts : 2 * experts, :] = weight[span]

    loads[0].wait()
    loads[1].wait()
    make_table()
    metas[me] = table[me]
    loads[2].wait()
    loads[3].wait()
    pl.semaphore_wait(barrier, groups)

    def meta_copy(to):
        return copy(table.at[to], metas.at[me], ms.at[to], mr.at[me], at(to))

    def meta_arrival(source):
        return copy(table.at[source], metas.at[source], ms.at[source], mr.at[source], at(source))

    def peer_of(step):
        return (flip(z, step, outer) * MID + x) * CORES + c

    def z_copy(step, part):
        return copy(ag[part].at[me], ag[part].at[me], zs.at[step, part], zr.at[step, part], at(peer_of(step)))

    def z_arrival(step, part):
        blk = peer_of(step)
        return copy(ag[part].at[blk], ag[part].at[blk], zs.at[step, part], zr.at[step, part], at(blk))

    def x_copy(step, part, blk):
        return copy(
            ag[part].at[blk], ag[part].at[blk], xs.at[step, part], xr.at[step, part], at(x_peer)
        )

    def c_copy(step, across, part, blk):
        return copy(
            ag[part].at[blk], ag[part].at[blk],
            cs.at[step, across, part], cr.at[step, across, part], at(core_peer),
        )

    def y_copy(u, part, e):
        return copy(
            ysend[part].at[u, e], yrecv[part].at[u, e], ys.at[u, part, e], yr.at[u, part, e], other_dp
        )

    def rc_copy(u, part):
        return copy(
            acc.at[part, 1 - c], crecv.at[u, part], rcs.at[u, part], rcr.at[u, part], at(core_peer)
        )

    def rx_copy(step, part):
        return copy(
            xsend.at[step, part], xrecv.at[step, part],
            rxs.at[step, part], rxr.at[step, part], at(x_peer),
        )

    def rz_copy(step, part):
        return copy(
            zsend.at[step, part], zrecv.at[step, part],
            rzs.at[step, part], rzr.at[step, part], at(peer_of(step)),
        )

    def step_of(u):
        g = lax.rem(lax.div(u + 1, 2), outer)
        return (lax.rem(g, outer - 1) + 1) * lax.div(g + outer - 1, outer)

    def across_of(u):
        first = 1 - lax.div(u + units - 1, units)
        last = lax.div(u + 1, units)
        swap = lax.div(u + 3, units) - lax.div(u + 1, units)
        flat = lax.rem(u + 1, 2)
        return flat + swap * (1 - 2 * flat) + last - first

    def base_of(u):
        across = across_of(u)
        return (flip(z, step_of(u), outer) * MID + x + across - 2 * x * across) * CORES

    order = [step for step in range(2, outer)] + [1]

    for part in range(2):
        c_copy(0, 0, part, me).start()
    meta_copy(core_peer).start()
    @pl.loop(1, groups)
    def _(k):
        to = lax.rem(me + k, groups)

        @pl.when(to != core_peer)
        def _():
            meta_copy(to).start()

    for part in range(2):
        z_copy(order[0], part).start()
    for part in range(2):
        x_copy(0, part, me).start()

    for part in range(2):
        for step in order[-1:] if outer > 2 else []:
            z_copy(step, part).start()

    def pick_of(u):
        base = base_of(u)
        tiles = metas[pl.ds(base, CORES)]
        slot = lax.broadcasted_iota(jnp.int32, (CORES * slots, CORES * rows), 0).astype(F32)
        picks, weights = [], []
        for e in range(experts):
            line = jnp.concatenate(
                [tiles[b, e : e + 1] + float(b * slots) for b in range(CORES)], axis=1
            )
            share = jnp.concatenate(
                [tiles[b, experts + e : experts + e + 1] for b in range(CORES)], axis=1
            )
            match = slot == line
            picks.append(jnp.where(match, 1.0, 0.0))
            weights.append(jnp.sum(jnp.where(match, share, 0.0), axis=1, keepdims=True))
        return jnp.concatenate(picks, axis=0), weights

    lines = CORES * slots

    def hand_on(step, part, col):
        z_arrival(step, part).wait_recv()
        x_copy(step, part, col).start()
        c_copy(step, 0, part, col).start()

    def first_half(i, u, part):
        step, across, base = step_of(u), across_of(u), base_of(u)
        col = base + c

        def arrive():
            @pl.when(across > 0)
            def _():
                x_copy(step, part, col).wait_recv()
                c_copy(step, 1, part, col).start()

            @pl.when(((1 - across) * step > 0) & (u != units - 2))
            def _():
                hand_on(step, part, col)

            c_copy(step, across, part, base + 1 - c).wait_recv()

        @pl.when(i < 2 * units)
        def _():
            arrive()

        @pl.when(i == 0)
        def _():
            meta_arrival(core_peer).wait_recv()
            weight(0, 0).wait()
            weight(1, 0).wait()

        @pl.when(i == 1)
        def _():
            weight(2, 0).wait()

        @pl.when(i == 2)
        def _():
            for e in range(1, experts):
                for which in range(3):
                    weight(which, e).wait()

            @pl.loop(1, groups)
            def _(k):
                source = lax.rem(me + k, groups)

                @pl.when(source != core_peer)
                def _():
                    meta_arrival(source).wait_recv()

        pick, _ = pick_of(u)
        block = ag[part][pl.ds(base, CORES)].reshape(CORES * rows, half)
        got = dot(pick.astype(BF16), block, ((1,), (0,))).astype(BF16)
        for e in range(experts):
            @pl.when((i < 2 * units) if e == 0 else (i >= 2))
            def _():
                mine = got[e * lines : (e + 1) * lines]
                if part == 0:
                    ysend_pre[u, e, :, :hid] = dot(mine, wg_ref[e], ((1,), (0,))).astype(BF16)
                    ysend_pre[u, e, :, hid:] = dot(mine, wu_ref[e], ((1,), (0,))).astype(BF16)
                else:
                    ysend_back[u, e] = dot(mine, wd_ref[e], ((1,), (1,))).astype(BF16)
                y_copy(u, part, e).start()

    def sums(u, e):
        def total(lo):
            piece = ysend_pre[u, e, :, lo : lo + hid].astype(F32)
            return piece + yrecv_pre[u, e, :, lo : lo + hid].astype(F32)

        return total(0), total(hid)

    def mixed_half(u, e, share):
        a, b = sums(u, e)
        act = (a * jax.nn.sigmoid(a) * b * share).astype(BF16)
        return dot(act, wd_ref[e], ((1,), (0,))).astype(BF16)

    def grad_half(u, e, share):
        a, b = sums(u, e)
        back = (ysend_back[u, e].astype(F32) + yrecv_back[u, e].astype(F32)) * share
        sig = jax.nn.sigmoid(a)
        d_gate = (back * b * sig * (1.0 + a * (1.0 - sig))).astype(BF16)
        d_up = (back * a * sig).astype(BF16)
        grad = dot(d_gate, wg_ref[e], ((1,), (1,))) + dot(d_up, wu_ref[e], ((1,), (1,)))
        return grad.astype(BF16)

    def to_x_peer(u, part):
        step, across = step_of(u), across_of(u)
        rc_copy(u, part).wait_recv()
        both = (acc[part, c].astype(F32) + crecv[u, part].astype(F32)).astype(BF16)

        @pl.when(across == 0)
        def _():
            hold[step, part] = both

        @pl.when(across > 0)
        def _():
            xsend[step, part] = both
            rx_copy(step, part).start()

        rc_copy(u, part).wait_send()

    def to_owner(step, part):
        rx_copy(step, part).wait_recv()
        here = hold[step, part].astype(F32) + xrecv[step, part].astype(F32)
        zsend[step, part] = here.astype(BF16)
        rz_copy(step, part).start()

    def item(i):
        first, second, third = same(i, 0), same(i, 1), same(i, 2)
        ends = [same(i, 2 * units + k) for k in (-1, 0, 1)]
        u = lax.div(i + 1, 2) - 1 + first + (units - 1) * (third - ends[1]) - units * ends[2]
        part = lax.rem(i + 1, 2) - first + second - third + ends[0] - ends[1] + ends[2]
        return u, part

    def second_half(i, u, part):
        step, before = step_of(u), step_of(u - 1 + lax.div(units - u, units))
        kept = lax.div(units - u, units)

        @pl.when((u > 1) & (u < units - 1) & (lax.rem(u, 2) == 1))
        def _():
            to_owner(before, part)

        pick, shares = pick_of(u)
        for e in range(experts):
            @pl.when((i < 2 * units) if e == 0 else (i >= 2))
            def _():
                y_copy(u, part, e).wait_recv()
                ready[kept, part, e] = (grad_half if part else mixed_half)(u, e, shares[e])

        @pl.when(i >= 2)
        def _():
            values = ready[kept, part].reshape(experts * lines, half)
            spread = dot(pick.T.astype(BF16), values, ((1,), (0,)))
            acc[part] = spread.astype(BF16).reshape(CORES, rows, half)
            rc_copy(u, part).start()

        @pl.when((i >= 2) & (i < 2 * units))
        def _():
            to_x_peer(u, part)

        @pl.when(u == units - 2)
        def _():
            to_owner(step, part)

    def out_copy(part):
        return pltpu.make_async_copy(zsend.at[0, part], outputs[part], osem.at[part])

    def finish(part):
        for step in order:
            rz_copy(step, part).wait_recv()
        rx_copy(0, part).wait_recv()
        final = xrecv[0, part].astype(F32)
        for step in order:
            final = final + zrecv[step, part].astype(F32)
        rc_copy(0, part).wait_recv()
        final = final + acc[part, c].astype(F32) + crecv[0, part].astype(F32)
        zsend[0, part] = final.astype(BF16)
        out_copy(part).start()

    @pl.loop(0, 2 * units + 2 + AHEAD)
    def _(i):
        @pl.when(i < 2 * units + 2)
        def _():
            u, part = item(i)
            for which in range(2):
                @pl.when(part == which)
                def _():
                    first_half(i, u, which)

            @pl.when(i == 2 * outer - 2)
            def _():
                for which in range(2):
                    hand_on(order[-1], which, peer_of(order[-1]))

            for later, step in enumerate(order[1:-1]):
                @pl.when(i == 4 * later + 4)
                def _():
                    for which in range(2):
                        z_copy(step, which).start()

        @pl.when(i >= AHEAD)
        def _():
            u, part = item(i - AHEAD)
            for which in range(2):
                @pl.when(part == which)
                def _():
                    second_half(i - AHEAD, u, which)

    finish(0)
    finish(1)

    @pl.loop(1, groups)
    def _(k):
        meta_copy(lax.rem(me + k, groups)).wait_send()

    for part in range(2):
        for step in range(outer):
            x_copy(step, part, me).wait_send()
            rx_copy(step, part).wait_send()
            for across in range(2):
                c_copy(step, across, part, me).wait_send()
            if step:
                z_copy(step, part).wait_send()
                rz_copy(step, part).wait_send()
        for u in range(units):
            for e in range(experts):
                y_copy(u, part, e).wait_send()
        rc_copy(0, part).wait_send()
        out_copy(part).wait()


def deliver(*parts):
    def move(a_ref, b_ref, c_ref, d_ref):
        c_ref[...] = a_ref[...]
        d_ref[...] = b_ref[...]

    spec = pl.BlockSpec(memory_space=pltpu.VMEM)
    return pl.pallas_call(
        move, out_shape=tuple(jax.ShapeDtypeStruct(p.shape, p.dtype) for p in parts),
        in_specs=[spec, spec], out_specs=(spec, spec),
    )(*parts)


def fused_device(soft_tokens, expert_ids, gate_mix, w_gate, w_up, w_down, out_grad):
    tok_rows, width_part = soft_tokens.shape
    top_count = expert_ids.shape[1]
    local_experts, _, hid = w_gate.shape
    groups = lax.axis_size("expert")
    experts = groups * local_experts
    capacity = max(2, tok_rows * top_count * 5 // (4 * experts))
    plane = MID * CORES
    outer = groups // plane
    units = 2 * outer
    lines = CORES * capacity
    hbm = pl.BlockSpec(memory_space=pl.ANY)
    dma = pltpu.SemaphoreType.DMA
    out = jax.ShapeDtypeStruct((tok_rows, width_part), BF16)
    table_rows = -(-2 * local_experts // 8) * 8
    block = (tok_rows, width_part)
    parts = pl.pallas_call(
        functools.partial(fused_kernel, groups, capacity),
        out_shape=(out, out),
        in_specs=[hbm] * 7,
        out_specs=(hbm, hbm),
        scratch_shapes=[
            pltpu.VMEM((top_count, tok_rows), jnp.int32),
            pltpu.VMEM((top_count, tok_rows), F32),
            pltpu.VMEM(w_gate.shape, BF16),
            pltpu.VMEM(w_up.shape, BF16),
            pltpu.VMEM(w_down.shape, BF16),
            pltpu.VMEM((groups, *block), BF16),
            pltpu.VMEM((groups, *block), BF16),
            pltpu.VMEM((groups, table_rows, tok_rows), F32),
            pltpu.VMEM((groups, table_rows, tok_rows), F32),
            pltpu.VMEM((units, local_experts, lines, 2 * hid), BF16),
            pltpu.VMEM((units, local_experts, lines, 2 * hid), BF16),
            pltpu.VMEM((units, local_experts, lines, hid), BF16),
            pltpu.VMEM((units, local_experts, lines, hid), BF16),
            pltpu.VMEM((2, 2, local_experts, lines, width_part), BF16),
            pltpu.VMEM((2, CORES, *block), BF16),
            pltpu.VMEM((units, 2, *block), BF16),
            pltpu.VMEM((outer, 2, *block), BF16),
            pltpu.VMEM((outer, 2, *block), BF16),
            pltpu.VMEM((outer, 2, *block), BF16),
            pltpu.VMEM((outer, 2, *block), BF16),
            pltpu.VMEM((outer, 2, *block), BF16),
            dma((4,)), dma((3, local_experts)), dma((2,)),
            dma((groups,)), dma((groups,)),
            dma((outer, 2)), dma((outer, 2)),
            dma((outer, 2)), dma((outer, 2)),
            dma((outer, 2, 2)), dma((outer, 2, 2)),
            dma((units, 2, local_experts)), dma((units, 2, local_experts)),
            dma((units, 2)), dma((units, 2)),
            dma((outer, 2)), dma((outer, 2)),
            dma((outer, 2)), dma((outer, 2)),
        ],
        compiler_params=pltpu.CompilerParams(
            collective_id=0, has_side_effects=True, vmem_limit_bytes=67043328
        ),
    )(soft_tokens, out_grad, expert_ids.T, gate_mix.T, w_gate, w_up, w_down)
    return deliver(*parts)


def solution(mesh):
    in_specs = (
        P("expert", "dp"),
        P("expert", None),
        P("expert", None),
        P("expert", "dp", None),
        P("expert", "dp", None),
        P("expert", None, "dp"),
        P("expert", "dp"),
    )
    out_specs = (P("expert", "dp"), P("expert", "dp"))
    fits = mesh.shape["dp"] == 2 and mesh.shape["expert"] in (8, 16)
    return jax.shard_map(
        fused_device if fits else per_device,
        mesh=mesh, in_specs=in_specs, out_specs=out_specs, check_vma=False,
    )
```

```python
import functools

import jax
import jax.numpy as jnp
from jax import lax
from jax.experimental import pallas as pl
from jax.experimental.pallas import tpu as pltpu
from jax.sharding import PartitionSpec as P

F32 = jnp.float32
BF16 = jnp.bfloat16


def slot_maps(ids, mix, first, local_experts, capacity):
    tok_rows = ids.shape[1]
    own = first + jnp.arange(local_experts, dtype=jnp.int32)
    hit = ids[:, None, :, :] == own[None, :, None, None]
    named = jnp.any(hit, axis=3)
    weight = jnp.sum(jnp.where(hit, mix[:, None, :, :], 0.0), axis=3)
    before = jnp.arange(tok_rows)[:, None] < jnp.arange(tok_rows)[None, :]
    place = jnp.einsum(
        "set,tu->seu", named.astype(BF16), before.astype(BF16), preferred_element_type=F32
    ).astype(jnp.int32)
    slots = jnp.arange(capacity, dtype=jnp.int32)
    pick = (place[:, :, None, :] == slots[None, None, :, None]) & named[:, :, None, :]
    slot_weight = jnp.sum(jnp.where(pick, weight[:, :, None, :], 0.0), axis=3)
    return pick.astype(BF16), slot_weight


def per_device(soft_tokens, expert_ids, gate_mix, w_gate, w_up, w_down, out_grad):
    tok_rows, width_part = soft_tokens.shape
    top_count = expert_ids.shape[1]
    local_experts = w_gate.shape[0]
    hidden = w_gate.shape[2]
    groups = lax.axis_size("expert")
    dp_count = lax.axis_size("dp")
    experts = groups * local_experts
    capacity = max(2, tok_rows * top_count * 5 // (4 * experts))
    both = lax.all_gather(jnp.concatenate([soft_tokens, out_grad], axis=1), "expert")
    ids = lax.all_gather(expert_ids, "expert")
    mix = lax.all_gather(gate_mix, "expert")
    first = lax.axis_index("expert") * local_experts
    pick, slot_weight = slot_maps(ids, mix, first, local_experts, capacity)
    rows = jnp.einsum("sect,std->secd", pick, both, preferred_element_type=F32).astype(BF16)
    pre = [
        jnp.einsum("secd,edf->secf", rows[..., :width_part], w, preferred_element_type=F32)
        for w in (w_gate, w_up)
    ]
    back = jnp.einsum("secd,efd->secf", rows[..., width_part:], w_down, preferred_element_type=F32)
    part = jnp.concatenate(pre + [back], axis=-1).astype(BF16)
    total = part.astype(F32)
    moved = part
    for _ in range(dp_count - 1):
        moved = lax.ppermute(moved, "dp", [(i, (i + 1) % dp_count) for i in range(dp_count)])
        total = total + moved.astype(F32)
    a = total[..., :hidden]
    b = total[..., hidden : 2 * hidden]
    back = total[..., 2 * hidden :] * slot_weight[..., None]
    sig = jax.nn.sigmoid(a)
    act = (a * sig * b * slot_weight[..., None]).astype(BF16)
    d_gate = (back * b * sig * (1.0 + a * (1.0 - sig))).astype(BF16)
    d_up = (back * a * sig).astype(BF16)
    out = jnp.einsum("secf,efd->secd", act, w_down, preferred_element_type=F32)
    grad = jnp.einsum("secf,edf->secd", d_gate, w_gate, preferred_element_type=F32) + jnp.einsum(
        "secf,edf->secd", d_up, w_up, preferred_element_type=F32
    )
    result = jnp.concatenate([out, grad], axis=-1).astype(BF16)
    spread = jnp.einsum("sect,secd->std", pick, result, preferred_element_type=F32).astype(BF16)
    summed = lax.psum_scatter(spread, "expert", scatter_dimension=0, tiled=False)
    return summed[:, :width_part], summed[:, width_part:]


MESH = pl.DeviceIdType.MESH
MID = 2
CORES = 2
AHEAD = 4


def same(a, b):
    gap = (a - b) * (a - b)
    return 1 - lax.div(2 * gap, gap + 1)


def flip(value, step, count):
    out, bit = 0, 1
    while bit < count:
        out = out + lax.rem(lax.div(value, bit) + lax.div(step, bit), 2) * bit
        bit *= 2
    return out


def fused_kernel(
    groups, slots, tok_hbm, cot_hbm, ids_hbm, mix_hbm, wg_hbm, wu_hbm, wd_hbm, mixed_hbm, tgrad_hbm,
    ids_ref, mix_ref, wg_ref, wu_ref, wd_ref, ag_tok, ag_cot, table, metas,
    ysend_pre, yrecv_pre, ysend_back, yrecv_back, ready, acc, crecv, hold, xsend, xrecv, zsend, zrecv,
    lsem, wsem, osem, ms, mr, zs, zr, xs, xr, cs, cr, ys, yr, rcs, rcr, rxs, rxr, rzs, rzr,
):
    rows, half = tok_hbm.shape
    experts, _, hid = wg_ref.shape
    plane = MID * CORES
    outer = groups // plane
    units = 2 * outer
    me = lax.axis_index("expert")
    y = lax.axis_index("dp")
    z = lax.div(me, plane)
    x = lax.rem(lax.div(me, CORES), MID)
    c = lax.rem(me, CORES)
    core_peer = (z * MID + x) * CORES + 1 - c
    x_peer = (z * MID + 1 - x) * CORES + c
    other_dp = {"dp": 1 - y, "expert": me}
    ag = (ag_tok, ag_cot)
    outputs = (mixed_hbm, tgrad_hbm)
    ysend, yrecv = (ysend_pre, ysend_back), (yrecv_pre, yrecv_back)

    def at(expert):
        return {"dp": y, "expert": expert}

    def copy(src, dst, send, recv, device):
        return pltpu.make_async_remote_copy(
            src_ref=src, dst_ref=dst, send_sem=send, recv_sem=recv,
            device_id=device, device_id_type=MESH,
        )

    barrier = pltpu.get_barrier_semaphore()
    for k in range(1, groups):
        pl.semaphore_signal(
            barrier, inc=1, device_id=at(lax.rem(me + k, groups)), device_id_type=MESH
        )
    pl.semaphore_signal(barrier, inc=1, device_id=other_dp, device_id_type=MESH)

    loads = [
        pltpu.make_async_copy(src, dst, lsem.at[k])
        for k, (src, dst) in enumerate(
            ((ids_hbm, ids_ref), (mix_hbm, mix_ref), (tok_hbm, ag_tok.at[me]), (cot_hbm, ag_cot.at[me]))
        )
    ]

    def weight(which, e):
        src, dst = ((wg_hbm, wg_ref), (wu_hbm, wu_ref), (wd_hbm, wd_ref))[which]
        return pltpu.make_async_copy(src.at[e], dst.at[e], wsem.at[which, e])

    for load in loads:
        load.start()
    for e in range(experts):
        for which in range(3):
            weight(which, e).start()

    def dot(a, b, dims):
        return lax.dot_general(a, b, (dims, ((), ())), preferred_element_type=F32)

    def make_table():
        total = groups * experts
        expert = lax.broadcasted_iota(jnp.int32, (total, rows), 0)
        named = jnp.zeros((total, rows), F32)
        weight = jnp.zeros((total, rows), F32)
        for k in range(ids_ref.shape[0]):
            hit = expert == ids_ref[k : k + 1, :]
            named = named + jnp.where(hit, 1.0, 0.0)
            weight = weight + jnp.where(hit, mix_ref[k : k + 1, :], 0.0)
        before = lax.broadcasted_iota(jnp.int32, (rows, rows), 0) < lax.broadcasted_iota(
            jnp.int32, (rows, rows), 1
        )
        before = jnp.where(before, 1.0, 0.0).astype(BF16)
        place = dot(named.astype(BF16), before, ((1,), (0,)))
        key = jnp.where(named > 0.0, place, -4.0 * slots)
        table[...] = jnp.zeros_like(table)
        for d in range(groups):
            span = slice(d * experts, (d + 1) * experts)
            table[d, :experts, :] = key[span]
            table[d, experts : 2 * experts, :] = weight[span]

    loads[0].wait()
    loads[1].wait()
    make_table()
    metas[me] = table[me]
    loads[2].wait()
    loads[3].wait()
    pl.semaphore_wait(barrier, groups)

    def meta_copy(to):
        return copy(table.at[to], metas.at[me], ms.at[to], mr.at[me], at(to))

    def meta_arrival(source):
        return copy(table.at[source], metas.at[source], ms.at[source], mr.at[source], at(source))

    def peer_of(step):
        return (flip(z, step, outer) * MID + x) * CORES + c

    def z_copy(step, part):
        return copy(ag[part].at[me], ag[part].at[me], zs.at[step, part], zr.at[step, part], at(peer_of(step)))

    def z_arrival(step, part):
        blk = peer_of(step)
        return copy(ag[part].at[blk], ag[part].at[blk], zs.at[step, part], zr.at[step, part], at(blk))

    def x_copy(step, part, blk):
        return copy(
            ag[part].at[blk], ag[part].at[blk], xs.at[step, part], xr.at[step, part], at(x_peer)
        )

    def c_copy(step, across, part, blk):
        return copy(
            ag[part].at[blk], ag[part].at[blk],
            cs.at[step, across, part], cr.at[step, across, part], at(core_peer),
        )

    def y_copy(u, part, e):
        return copy(
            ysend[part].at[u, e], yrecv[part].at[u, e], ys.at[u, part, e], yr.at[u, part, e], other_dp
        )

    def rc_copy(u, part):
        return copy(
            acc.at[part, 1 - c], crecv.at[u, part], rcs.at[u, part], rcr.at[u, part], at(core_peer)
        )

    def rx_copy(step, part):
        return copy(
            xsend.at[step, part], xrecv.at[step, part],
            rxs.at[step, part], rxr.at[step, part], at(x_peer),
        )

    def rz_copy(step, part):
        return copy(
            zsend.at[step, part], zrecv.at[step, part],
            rzs.at[step, part], rzr.at[step, part], at(peer_of(step)),
        )

    def step_of(u):
        g = lax.rem(lax.div(u + 1, 2), outer)
        return (lax.rem(g, outer - 1) + 1) * lax.div(g + outer - 1, outer)

    def across_of(u):
        first = 1 - lax.div(u + units - 1, units)
        last = lax.div(u + 1, units)
        swap = lax.div(u + 3, units) - lax.div(u + 1, units)
        flat = lax.rem(u + 1, 2)
        return flat + swap * (1 - 2 * flat) + last - first

    def base_of(u):
        across = across_of(u)
        return (flip(z, step_of(u), outer) * MID + x + across - 2 * x * across) * CORES

    order = [step for step in range(2, outer)] + [1]

    for part in range(2):
        c_copy(0, 0, part, me).start()
    meta_copy(core_peer).start()
    @pl.loop(1, groups)
    def _(k):
        to = lax.rem(me + k, groups)

        @pl.when(to != core_peer)
        def _():
            meta_copy(to).start()

    for part in range(2):
        z_copy(order[0], part).start()
    for part in range(2):
        x_copy(0, part, me).start()

    for part in range(2):
        for step in order[-1:] if outer > 2 else []:
            z_copy(step, part).start()

    def pick_of(u):
        base = base_of(u)
        tiles = metas[pl.ds(base, CORES)]
        slot = lax.broadcasted_iota(jnp.int32, (CORES * slots, CORES * rows), 0).astype(F32)
        picks, weights = [], []
        for e in range(experts):
            line = jnp.concatenate(
                [tiles[b, e : e + 1] + float(b * slots) for b in range(CORES)], axis=1
            )
            share = jnp.concatenate(
                [tiles[b, experts + e : experts + e + 1] for b in range(CORES)], axis=1
            )
            match = slot == line
            picks.append(jnp.where(match, 1.0, 0.0))
            weights.append(jnp.sum(jnp.where(match, share, 0.0), axis=1, keepdims=True))
        return jnp.concatenate(picks, axis=0), weights

    lines = CORES * slots

    def hand_on(step, part, col):
        z_arrival(step, part).wait_recv()
        x_copy(step, part, col).start()
        c_copy(step, 0, part, col).start()

    def first_half(i, u, part):
        step, across, base = step_of(u), across_of(u), base_of(u)
        col = base + c

        def arrive():
            @pl.when(across > 0)
            def _():
                x_copy(step, part, col).wait_recv()
                c_copy(step, 1, part, col).start()

            @pl.when(((1 - across) * step > 0) & (u != units - 2))
            def _():
                hand_on(step, part, col)

            c_copy(step, across, part, base + 1 - c).wait_recv()

        @pl.when(i < 2 * units)
        def _():
            arrive()

            if part == 0:
                for b in range(CORES):
                    @pl.when(base + b != me)
                    def _():
                        meta_arrival(base + b).wait_recv()

        @pl.when(i == 0)
        def _():
            weight(0, 0).wait()
            weight(1, 0).wait()

        @pl.when(i == 1)
        def _():
            weight(2, 0).wait()

        @pl.when(i == 2)
        def _():
            for e in range(1, experts):
                for which in range(3):
                    weight(which, e).wait()

        pick, _ = pick_of(u)
        block = ag[part][pl.ds(base, CORES)].reshape(CORES * rows, half)
        got = dot(pick.astype(BF16), block, ((1,), (0,))).astype(BF16)
        for e in range(experts):
            @pl.when((i < 2 * units) if e == 0 else (i >= 2))
            def _():
                mine = got[e * lines : (e + 1) * lines]
                if part == 0:
                    ysend_pre[u, e, :, :hid] = dot(mine, wg_ref[e], ((1,), (0,))).astype(BF16)
                    ysend_pre[u, e, :, hid:] = dot(mine, wu_ref[e], ((1,), (0,))).astype(BF16)
                else:
                    ysend_back[u, e] = dot(mine, wd_ref[e], ((1,), (1,))).astype(BF16)
                y_copy(u, part, e).start()

    def sums(u, e):
        def total(lo):
            piece = ysend_pre[u, e, :, lo : lo + hid].astype(F32)
            return piece + yrecv_pre[u, e, :, lo : lo + hid].astype(F32)

        return total(0), total(hid)

    def mixed_half(u, e, share):
        a, b = sums(u, e)
        act = (a * jax.nn.sigmoid(a) * b * share).astype(BF16)
        return dot(act, wd_ref[e], ((1,), (0,))).astype(BF16)

    def grad_half(u, e, share):
        a, b = sums(u, e)
        back = (ysend_back[u, e].astype(F32) + yrecv_back[u, e].astype(F32)) * share
        sig = jax.nn.sigmoid(a)
        d_gate = (back * b * sig * (1.0 + a * (1.0 - sig))).astype(BF16)
        d_up = (back * a * sig).astype(BF16)
        grad = dot(d_gate, wg_ref[e], ((1,), (1,))) + dot(d_up, wu_ref[e], ((1,), (1,)))
        return grad.astype(BF16)

    def to_x_peer(u, part):
        step, across = step_of(u), across_of(u)
        rc_copy(u, part).wait_recv()
        both = (acc[part, c].astype(F32) + crecv[u, part].astype(F32)).astype(BF16)

        @pl.when(across == 0)
        def _():
            hold[step, part] = both

        @pl.when(across > 0)
        def _():
            xsend[step, part] = both
            rx_copy(step, part).start()

        rc_copy(u, part).wait_send()

    def to_owner(step, part):
        rx_copy(step, part).wait_recv()
        here = hold[step, part].astype(F32) + xrecv[step, part].astype(F32)
        zsend[step, part] = here.astype(BF16)
        rz_copy(step, part).start()

    def item(i):
        pair = lax.div(i, 2)
        moved = (units - 1) * (same(pair, 1) - same(pair, units))
        u, part = pair - 1 + same(pair, 0) + moved, lax.rem(i, 2)
        return u, part

    def second_half(i, u, part):
        step, before = step_of(u), step_of(u - 1 + lax.div(units - u, units))
        kept = lax.div(units - u, units)

        @pl.when((u > 1) & (u < units - 1) & (lax.rem(u, 2) == 1))
        def _():
            to_owner(before, part)

        pick, shares = pick_of(u)
        for e in range(experts):
            @pl.when((i < 2 * units) if e == 0 else (i >= 2))
            def _():
                y_copy(u, part, e).wait_recv()
                ready[kept, part, e] = (grad_half if part else mixed_half)(u, e, shares[e])

        @pl.when(i >= 2)
        def _():
            values = ready[kept, part].reshape(experts * lines, half)
            spread = dot(pick.T.astype(BF16), values, ((1,), (0,)))
            acc[part] = spread.astype(BF16).reshape(CORES, rows, half)
            rc_copy(u, part).start()

        @pl.when((i >= 2) & (i < 2 * units))
        def _():
            to_x_peer(u, part)

        @pl.when(u == units - 2)
        def _():
            to_owner(step, part)

    def out_copy(part):
        return pltpu.make_async_copy(zsend.at[0, part], outputs[part], osem.at[part])

    def finish(part):
        for step in order:
            rz_copy(step, part).wait_recv()
        rx_copy(0, part).wait_recv()
        final = xrecv[0, part].astype(F32)
        for step in order:
            final = final + zrecv[step, part].astype(F32)
        rc_copy(0, part).wait_recv()
        final = final + acc[part, c].astype(F32) + crecv[0, part].astype(F32)
        outputs[part][...] = final.astype(BF16)

    @pl.loop(0, 2 * units + 2 + AHEAD)
    def _(i):
        @pl.when(i < 2 * units + 2)
        def _():
            u, part = item(i)
            for which in range(2):
                @pl.when(part == which)
                def _():
                    first_half(i, u, which)

            @pl.when(i == 2 * outer - 1)
            def _():
                for which in range(2):
                    hand_on(order[-1], which, peer_of(order[-1]))

            for later, step in enumerate(order[1:-1]):
                @pl.when(i == 4 * later + 5)
                def _():
                    for which in range(2):
                        z_copy(step, which).start()

        @pl.when(i >= AHEAD)
        def _():
            u, part = item(i - AHEAD)
            for which in range(2):
                @pl.when(part == which)
                def _():
                    second_half(i - AHEAD, u, which)

    finish(0)
    finish(1)

    @pl.loop(1, groups)
    def _(k):
        meta_copy(lax.rem(me + k, groups)).wait_send()

    for part in range(2):
        for step in range(outer):
            x_copy(step, part, me).wait_send()
            rx_copy(step, part).wait_send()
            for across in range(2):
                c_copy(step, across, part, me).wait_send()
            if step:
                z_copy(step, part).wait_send()
                rz_copy(step, part).wait_send()
        for u in range(units):
            for e in range(experts):
                y_copy(u, part, e).wait_send()
        rc_copy(0, part).wait_send()


def fused_device(soft_tokens, expert_ids, gate_mix, w_gate, w_up, w_down, out_grad):
    tok_rows, width_part = soft_tokens.shape
    top_count = expert_ids.shape[1]
    local_experts, _, hid = w_gate.shape
    groups = lax.axis_size("expert")
    experts = groups * local_experts
    capacity = max(2, tok_rows * top_count * 5 // (4 * experts))
    plane = MID * CORES
    outer = groups // plane
    units = 2 * outer
    lines = CORES * capacity
    hbm = pl.BlockSpec(memory_space=pl.ANY)
    dma = pltpu.SemaphoreType.DMA
    out = pltpu.VMEM((tok_rows, width_part), BF16)
    table_rows = -(-2 * local_experts // 8) * 8
    block = (tok_rows, width_part)
    return pl.pallas_call(
        functools.partial(fused_kernel, groups, capacity),
        out_shape=(out, out),
        in_specs=[hbm] * 7,
        out_specs=(pl.BlockSpec(memory_space=pltpu.VMEM),) * 2,
        scratch_shapes=[
            pltpu.VMEM((top_count, tok_rows), jnp.int32),
            pltpu.VMEM((top_count, tok_rows), F32),
            pltpu.VMEM(w_gate.shape, BF16),
            pltpu.VMEM(w_up.shape, BF16),
            pltpu.VMEM(w_down.shape, BF16),
            pltpu.VMEM((groups, *block), BF16),
            pltpu.VMEM((groups, *block), BF16),
            pltpu.VMEM((groups, table_rows, tok_rows), F32),
            pltpu.VMEM((groups, table_rows, tok_rows), F32),
            pltpu.VMEM((units, local_experts, lines, 2 * hid), BF16),
            pltpu.VMEM((units, local_experts, lines, 2 * hid), BF16),
            pltpu.VMEM((units, local_experts, lines, hid), BF16),
            pltpu.VMEM((units, local_experts, lines, hid), BF16),
            pltpu.VMEM((2, 2, local_experts, lines, width_part), BF16),
            pltpu.VMEM((2, CORES, *block), BF16),
            pltpu.VMEM((units, 2, *block), BF16),
            pltpu.VMEM((outer, 2, *block), BF16),
            pltpu.VMEM((outer, 2, *block), BF16),
            pltpu.VMEM((outer, 2, *block), BF16),
            pltpu.VMEM((outer, 2, *block), BF16),
            pltpu.VMEM((outer, 2, *block), BF16),
            dma((4,)), dma((3, local_experts)), dma((2,)),
            dma((groups,)), dma((groups,)),
            dma((outer, 2)), dma((outer, 2)),
            dma((outer, 2)), dma((outer, 2)),
            dma((outer, 2, 2)), dma((outer, 2, 2)),
            dma((units, 2, local_experts)), dma((units, 2, local_experts)),
            dma((units, 2)), dma((units, 2)),
            dma((outer, 2)), dma((outer, 2)),
            dma((outer, 2)), dma((outer, 2)),
        ],
        compiler_params=pltpu.CompilerParams(
            collective_id=0, has_side_effects=True, vmem_limit_bytes=60 * 1024 * 1024
        ),
    )(soft_tokens, out_grad, expert_ids.T, gate_mix.T, w_gate, w_up, w_down)


def solution(mesh):
    in_specs = (
        P("expert", "dp"),
        P("expert", None),
        P("expert", None),
        P("expert", "dp", None),
        P("expert", "dp", None),
        P("expert", None, "dp"),
        P("expert", "dp"),
    )
    out_specs = (P("expert", "dp"), P("expert", "dp"))
    fits = mesh.shape["dp"] == 2 and mesh.shape["expert"] in (8, 16)
    return jax.shard_map(
        fused_device if fits else per_device,
        mesh=mesh, in_specs=in_specs, out_specs=out_specs, check_vma=False,
    )
```

```python
import functools

import jax
import jax.numpy as jnp
from jax import lax
from jax.experimental import pallas as pl
from jax.experimental.pallas import tpu as pltpu
from jax.sharding import PartitionSpec as P

F32 = jnp.float32
BF16 = jnp.bfloat16


def slot_maps(ids, mix, first, local_experts, capacity):
    tok_rows = ids.shape[1]
    own = first + jnp.arange(local_experts, dtype=jnp.int32)
    hit = ids[:, None, :, :] == own[None, :, None, None]
    named = jnp.any(hit, axis=3)
    weight = jnp.sum(jnp.where(hit, mix[:, None, :, :], 0.0), axis=3)
    before = jnp.arange(tok_rows)[:, None] < jnp.arange(tok_rows)[None, :]
    place = jnp.einsum(
        "set,tu->seu", named.astype(BF16), before.astype(BF16), preferred_element_type=F32
    ).astype(jnp.int32)
    slots = jnp.arange(capacity, dtype=jnp.int32)
    pick = (place[:, :, None, :] == slots[None, None, :, None]) & named[:, :, None, :]
    slot_weight = jnp.sum(jnp.where(pick, weight[:, :, None, :], 0.0), axis=3)
    return pick.astype(BF16), slot_weight


def per_device(soft_tokens, expert_ids, gate_mix, w_gate, w_up, w_down, out_grad):
    tok_rows, width_part = soft_tokens.shape
    top_count = expert_ids.shape[1]
    local_experts = w_gate.shape[0]
    hidden = w_gate.shape[2]
    groups = lax.axis_size("expert")
    dp_count = lax.axis_size("dp")
    experts = groups * local_experts
    capacity = max(2, tok_rows * top_count * 5 // (4 * experts))
    both = lax.all_gather(jnp.concatenate([soft_tokens, out_grad], axis=1), "expert")
    ids = lax.all_gather(expert_ids, "expert")
    mix = lax.all_gather(gate_mix, "expert")
    first = lax.axis_index("expert") * local_experts
    pick, slot_weight = slot_maps(ids, mix, first, local_experts, capacity)
    rows = jnp.einsum("sect,std->secd", pick, both, preferred_element_type=F32).astype(BF16)
    pre = [
        jnp.einsum("secd,edf->secf", rows[..., :width_part], w, preferred_element_type=F32)
        for w in (w_gate, w_up)
    ]
    back = jnp.einsum("secd,efd->secf", rows[..., width_part:], w_down, preferred_element_type=F32)
    part = jnp.concatenate(pre + [back], axis=-1).astype(BF16)
    total = part.astype(F32)
    moved = part
    for _ in range(dp_count - 1):
        moved = lax.ppermute(moved, "dp", [(i, (i + 1) % dp_count) for i in range(dp_count)])
        total = total + moved.astype(F32)
    a = total[..., :hidden]
    b = total[..., hidden : 2 * hidden]
    back = total[..., 2 * hidden :] * slot_weight[..., None]
    sig = jax.nn.sigmoid(a)
    act = (a * sig * b * slot_weight[..., None]).astype(BF16)
    d_gate = (back * b * sig * (1.0 + a * (1.0 - sig))).astype(BF16)
    d_up = (back * a * sig).astype(BF16)
    out = jnp.einsum("secf,efd->secd", act, w_down, preferred_element_type=F32)
    grad = jnp.einsum("secf,edf->secd", d_gate, w_gate, preferred_element_type=F32) + jnp.einsum(
        "secf,edf->secd", d_up, w_up, preferred_element_type=F32
    )
    result = jnp.concatenate([out, grad], axis=-1).astype(BF16)
    spread = jnp.einsum("sect,secd->std", pick, result, preferred_element_type=F32).astype(BF16)
    summed = lax.psum_scatter(spread, "expert", scatter_dimension=0, tiled=False)
    return summed[:, :width_part], summed[:, width_part:]


MESH = pl.DeviceIdType.MESH
MID = 2
CORES = 2
AHEAD = 4


def same(a, b):
    gap = (a - b) * (a - b)
    return 1 - lax.div(2 * gap, gap + 1)


def flip(value, step, count):
    out, bit = 0, 1
    while bit < count:
        out = out + lax.rem(lax.div(value, bit) + lax.div(step, bit), 2) * bit
        bit *= 2
    return out


def fused_kernel(
    groups, slots, tok_hbm, cot_hbm, ids_hbm, mix_hbm, wg_hbm, wu_hbm, wd_hbm, mixed_hbm, tgrad_hbm,
    ids_ref, mix_ref, wg_ref, wu_ref, wd_ref, ag_tok, ag_cot, table, metas,
    ysend_pre, yrecv_pre, ysend_back, yrecv_back, ready, acc, crecv, hold, xsend, xrecv, zsend, zrecv,
    lsem, wsem, osem, ms, mr, zs, zr, xs, xr, cs, cr, ys, yr, rcs, rcr, rxs, rxr, rzs, rzr,
):
    rows, half = tok_hbm.shape
    experts, _, hid = wg_ref.shape
    plane = MID * CORES
    outer = groups // plane
    units = 2 * outer
    me = lax.axis_index("expert")
    y = lax.axis_index("dp")
    z = lax.div(me, plane)
    x = lax.rem(lax.div(me, CORES), MID)
    c = lax.rem(me, CORES)
    core_peer = (z * MID + x) * CORES + 1 - c
    x_peer = (z * MID + 1 - x) * CORES + c
    other_dp = {"dp": 1 - y, "expert": me}
    ag = (ag_tok, ag_cot)
    outputs = (mixed_hbm, tgrad_hbm)
    ysend, yrecv = (ysend_pre, ysend_back), (yrecv_pre, yrecv_back)

    def at(expert):
        return {"dp": y, "expert": expert}

    def copy(src, dst, send, recv, device):
        return pltpu.make_async_remote_copy(
            src_ref=src, dst_ref=dst, send_sem=send, recv_sem=recv,
            device_id=device, device_id_type=MESH,
        )

    barrier = pltpu.get_barrier_semaphore()
    for k in range(1, groups):
        pl.semaphore_signal(
            barrier, inc=1, device_id=at(lax.rem(me + k, groups)), device_id_type=MESH
        )
    pl.semaphore_signal(barrier, inc=1, device_id=other_dp, device_id_type=MESH)

    loads = [
        pltpu.make_async_copy(src, dst, lsem.at[k])
        for k, (src, dst) in enumerate(
            ((ids_hbm, ids_ref), (mix_hbm, mix_ref), (tok_hbm, ag_tok.at[me]), (cot_hbm, ag_cot.at[me]))
        )
    ]

    def weight(which, e):
        src, dst = ((wg_hbm, wg_ref), (wu_hbm, wu_ref), (wd_hbm, wd_ref))[which]
        return pltpu.make_async_copy(src.at[e], dst.at[e], wsem.at[which, e])

    for load in loads:
        load.start()
    for e in range(experts):
        for which in range(3):
            weight(which, e).start()

    def dot(a, b, dims):
        return lax.dot_general(a, b, (dims, ((), ())), preferred_element_type=F32)

    def make_table():
        total = groups * experts
        expert = lax.broadcasted_iota(jnp.int32, (total, rows), 0)
        named = jnp.zeros((total, rows), F32)
        weight = jnp.zeros((total, rows), F32)
        for k in range(ids_ref.shape[0]):
            hit = expert == ids_ref[k : k + 1, :]
            named = named + jnp.where(hit, 1.0, 0.0)
            weight = weight + jnp.where(hit, mix_ref[k : k + 1, :], 0.0)
        before = lax.broadcasted_iota(jnp.int32, (rows, rows), 0) < lax.broadcasted_iota(
            jnp.int32, (rows, rows), 1
        )
        before = jnp.where(before, 1.0, 0.0).astype(BF16)
        place = dot(named.astype(BF16), before, ((1,), (0,)))
        key = jnp.where(named > 0.0, place, -4.0 * slots)
        table[...] = jnp.zeros_like(table)
        for d in range(groups):
            span = slice(d * experts, (d + 1) * experts)
            table[d, :experts, :] = key[span]
            table[d, experts : 2 * experts, :] = weight[span]

    loads[0].wait()
    loads[1].wait()
    make_table()
    metas[me] = table[me]
    loads[2].wait()
    loads[3].wait()
    pl.semaphore_wait(barrier, groups)

    def meta_copy(to):
        return copy(table.at[to], metas.at[me], ms.at[to], mr.at[me], at(to))

    def meta_arrival(source):
        return copy(table.at[source], metas.at[source], ms.at[source], mr.at[source], at(source))

    def peer_of(step):
        return (flip(z, step, outer) * MID + x) * CORES + c

    def z_copy(step, part):
        return copy(ag[part].at[me], ag[part].at[me], zs.at[step, part], zr.at[step, part], at(peer_of(step)))

    def z_arrival(step, part):
        blk = peer_of(step)
        return copy(ag[part].at[blk], ag[part].at[blk], zs.at[step, part], zr.at[step, part], at(blk))

    def x_copy(step, part, blk):
        return copy(
            ag[part].at[blk], ag[part].at[blk], xs.at[step, part], xr.at[step, part], at(x_peer)
        )

    def c_copy(step, across, part, blk):
        return copy(
            ag[part].at[blk], ag[part].at[blk],
            cs.at[step, across, part], cr.at[step, across, part], at(core_peer),
        )

    def y_copy(u, part, e):
        return copy(
            ysend[part].at[u, e], yrecv[part].at[u, e], ys.at[u, part, e], yr.at[u, part, e], other_dp
        )

    def rc_copy(u, part):
        return copy(
            acc.at[part, 1 - c], crecv.at[u, part], rcs.at[u, part], rcr.at[u, part], at(core_peer)
        )

    def rx_copy(step, part):
        return copy(
            xsend.at[step, part], xrecv.at[step, part],
            rxs.at[step, part], rxr.at[step, part], at(x_peer),
        )

    def rz_copy(step, part):
        return copy(
            zsend.at[step, part], zrecv.at[step, part],
            rzs.at[step, part], rzr.at[step, part], at(peer_of(step)),
        )

    def step_of(u):
        g = lax.rem(lax.div(u + 1, 2), outer)
        return (lax.rem(g, outer - 1) + 1) * lax.div(g + outer - 1, outer)

    def across_of(u):
        first = 1 - lax.div(u + units - 1, units)
        last = lax.div(u + 1, units)
        swap = lax.div(u + 3, units) - lax.div(u + 1, units)
        flat = lax.rem(u + 1, 2)
        return flat + swap * (1 - 2 * flat) + last - first

    def base_of(u):
        across = across_of(u)
        return (flip(z, step_of(u), outer) * MID + x + across - 2 * x * across) * CORES

    order = [step for step in range(2, outer)] + [1]

    for part in range(2):
        c_copy(0, 0, part, me).start()
    meta_copy(core_peer).start()
    @pl.loop(1, groups)
    def _(k):
        to = lax.rem(me + k, groups)

        @pl.when(to != core_peer)
        def _():
            meta_copy(to).start()

    for part in range(2):
        z_copy(order[0], part).start()
    for part in range(2):
        x_copy(0, part, me).start()

    for part in range(2):
        for step in order[-1:] if outer > 2 else []:
            z_copy(step, part).start()

    def pick_of(u):
        base = base_of(u)
        tiles = metas[pl.ds(base, CORES)]
        slot = lax.broadcasted_iota(jnp.int32, (CORES * slots, CORES * rows), 0).astype(F32)
        picks, weights = [], []
        for e in range(experts):
            line = jnp.concatenate(
                [tiles[b, e : e + 1] + float(b * slots) for b in range(CORES)], axis=1
            )
            share = jnp.concatenate(
                [tiles[b, experts + e : experts + e + 1] for b in range(CORES)], axis=1
            )
            match = slot == line
            picks.append(jnp.where(match, 1.0, 0.0))
            weights.append(jnp.sum(jnp.where(match, share, 0.0), axis=1, keepdims=True))
        return jnp.concatenate(picks, axis=0), weights

    lines = CORES * slots

    def hand_on(step, part, col):
        z_arrival(step, part).wait_recv()
        x_copy(step, part, col).start()
        c_copy(step, 0, part, col).start()

    def first_half(i, u, part):
        step, across, base = step_of(u), across_of(u), base_of(u)
        col = base + c

        def arrive():
            @pl.when(across > 0)
            def _():
                x_copy(step, part, col).wait_recv()
                c_copy(step, 1, part, col).start()

            @pl.when(((1 - across) * step > 0) & (u != units - 2))
            def _():
                hand_on(step, part, col)

            c_copy(step, across, part, base + 1 - c).wait_recv()

        @pl.when(i < 2 * units)
        def _():
            arrive()

            if part == 0:
                for b in range(CORES):
                    @pl.when(base + b != me)
                    def _():
                        meta_arrival(base + b).wait_recv()

        @pl.when(i == 0)
        def _():
            weight(0, 0).wait()
            weight(1, 0).wait()

        @pl.when(i == 1)
        def _():
            weight(2, 0).wait()

        @pl.when(i == 2)
        def _():
            for e in range(1, experts):
                for which in range(3):
                    weight(which, e).wait()

        pick, _ = pick_of(u)
        block = ag[part][pl.ds(base, CORES)].reshape(CORES * rows, half)
        got = dot(pick.astype(BF16), block, ((1,), (0,))).astype(BF16)
        for e in range(experts):
            @pl.when((i < 2 * units) if e == 0 else (i >= 2))
            def _():
                mine = got[e * lines : (e + 1) * lines]
                if part == 0:
                    ysend_pre[u, e, :, :hid] = dot(mine, wg_ref[e], ((1,), (0,))).astype(BF16)
                    ysend_pre[u, e, :, hid:] = dot(mine, wu_ref[e], ((1,), (0,))).astype(BF16)
                else:
                    ysend_back[u, e] = dot(mine, wd_ref[e], ((1,), (1,))).astype(BF16)
                y_copy(u, part, e).start()

    def sums(u, e):
        def total(lo):
            piece = ysend_pre[u, e, :, lo : lo + hid].astype(F32)
            return piece + yrecv_pre[u, e, :, lo : lo + hid].astype(F32)

        return total(0), total(hid)

    def mixed_half(u, e, share):
        y_copy(u, 0, e).wait_recv()
        a, b = sums(u, e)
        act = (a * jax.nn.sigmoid(a) * b * share).astype(BF16)
        return dot(act, wd_ref[e], ((1,), (0,))).astype(BF16)

    def grad_half(u, e, share):
        a, b = sums(u, e)
        sig = jax.nn.sigmoid(a)
        by_gate = b * sig * (1.0 + a * (1.0 - sig))
        by_up = a * sig
        y_copy(u, 1, e).wait_recv()
        back = (ysend_back[u, e].astype(F32) + yrecv_back[u, e].astype(F32)) * share
        d_gate = (back * by_gate).astype(BF16)
        d_up = (back * by_up).astype(BF16)
        grad = dot(d_gate, wg_ref[e], ((1,), (1,))) + dot(d_up, wu_ref[e], ((1,), (1,)))
        return grad.astype(BF16)

    def to_x_peer(u, part):
        step, across = step_of(u), across_of(u)
        rc_copy(u, part).wait_recv()
        both = (acc[part, c].astype(F32) + crecv[u, part].astype(F32)).astype(BF16)

        @pl.when(across == 0)
        def _():
            hold[step, part] = both

        @pl.when(across > 0)
        def _():
            xsend[step, part] = both
            rx_copy(step, part).start()

        rc_copy(u, part).wait_send()

    def to_owner(step, part):
        rx_copy(step, part).wait_recv()
        here = hold[step, part].astype(F32) + xrecv[step, part].astype(F32)
        zsend[step, part] = here.astype(BF16)
        rz_copy(step, part).start()

    def item(i):
        pair = lax.div(i, 2)
        moved = (units - 1) * (same(pair, 1) - same(pair, units))
        u, part = pair - 1 + same(pair, 0) + moved, lax.rem(i, 2)
        return u, part

    def second_half(i, u, part):
        step, before = step_of(u), step_of(u - 1 + lax.div(units - u, units))
        kept = lax.div(units - u, units)

        @pl.when((u > 1) & (u < units - 1) & (lax.rem(u, 2) == 1))
        def _():
            to_owner(before, part)

        pick, shares = pick_of(u)
        spread_by = pick.T.astype(BF16)
        for e in range(experts):
            @pl.when((i < 2 * units) if e == 0 else (i >= 2))
            def _():
                ready[kept, part, e] = (grad_half if part else mixed_half)(u, e, shares[e])

        @pl.when(i >= 2)
        def _():
            values = ready[kept, part].reshape(experts * lines, half)
            spread = dot(spread_by, values, ((1,), (0,)))
            acc[part] = spread.astype(BF16).reshape(CORES, rows, half)
            rc_copy(u, part).start()

        @pl.when((i >= 2) & (i < 2 * units))
        def _():
            to_x_peer(u, part)

        @pl.when(u == units - 2)
        def _():
            to_owner(step, part)

    def out_copy(part):
        return pltpu.make_async_copy(zsend.at[0, part], outputs[part], osem.at[part])

    def finish(part):
        for step in order:
            rz_copy(step, part).wait_recv()
        rx_copy(0, part).wait_recv()
        final = xrecv[0, part].astype(F32)
        for step in order:
            final = final + zrecv[step, part].astype(F32)
        rc_copy(0, part).wait_recv()
        final = final + acc[part, c].astype(F32) + crecv[0, part].astype(F32)
        outputs[part][...] = final.astype(BF16)

    @pl.loop(0, 2 * units + 2 + AHEAD)
    def _(i):
        @pl.when(i < 2 * units + 2)
        def _():
            u, part = item(i)
            for which in range(2):
                @pl.when(part == which)
                def _():
                    first_half(i, u, which)

            @pl.when(i == 2 * outer - 1)
            def _():
                for which in range(2):
                    hand_on(order[-1], which, peer_of(order[-1]))

            for later, step in enumerate(order[1:-1]):
                @pl.when(i == 4 * later + 5)
                def _():
                    for which in range(2):
                        z_copy(step, which).start()

        @pl.when(i >= AHEAD)
        def _():
            u, part = item(i - AHEAD)
            for which in range(2):
                @pl.when(part == which)
                def _():
                    second_half(i - AHEAD, u, which)

    finish(0)
    finish(1)

    @pl.loop(1, groups)
    def _(k):
        meta_copy(lax.rem(me + k, groups)).wait_send()

    for part in range(2):
        for step in range(outer):
            x_copy(step, part, me).wait_send()
            rx_copy(step, part).wait_send()
            for across in range(2):
                c_copy(step, across, part, me).wait_send()
            if step:
                z_copy(step, part).wait_send()
                rz_copy(step, part).wait_send()
        for u in range(units):
            for e in range(experts):
                y_copy(u, part, e).wait_send()
        rc_copy(0, part).wait_send()


def deliver(*parts):
    def move(a_ref, b_ref, c_ref, d_ref, sem):
        copies = [
            pltpu.make_async_copy(src, dst, sem.at[k])
            for k, (src, dst) in enumerate(((a_ref, c_ref), (b_ref, d_ref)))
        ]
        for one in copies:
            one.start()
        for one in copies:
            one.wait()

    return pl.pallas_call(
        move, out_shape=tuple(jax.ShapeDtypeStruct(p.shape, p.dtype) for p in parts),
        in_specs=[pl.BlockSpec(memory_space=pltpu.VMEM)] * 2,
        out_specs=(pl.BlockSpec(memory_space=pl.ANY),) * 2,
        scratch_shapes=[pltpu.SemaphoreType.DMA((2,))],
    )(*(pltpu.with_memory_space_constraint(p, pltpu.VMEM) for p in parts))


def fused_device(soft_tokens, expert_ids, gate_mix, w_gate, w_up, w_down, out_grad):
    tok_rows, width_part = soft_tokens.shape
    top_count = expert_ids.shape[1]
    local_experts, _, hid = w_gate.shape
    groups = lax.axis_size("expert")
    experts = groups * local_experts
    capacity = max(2, tok_rows * top_count * 5 // (4 * experts))
    plane = MID * CORES
    outer = groups // plane
    units = 2 * outer
    lines = CORES * capacity
    hbm = pl.BlockSpec(memory_space=pl.ANY)
    dma = pltpu.SemaphoreType.DMA
    out = pltpu.VMEM((tok_rows, width_part), BF16)
    table_rows = -(-2 * local_experts // 8) * 8
    block = (tok_rows, width_part)
    parts = pl.pallas_call(
        functools.partial(fused_kernel, groups, capacity),
        out_shape=(out, out),
        in_specs=[hbm] * 7,
        out_specs=(pl.BlockSpec(memory_space=pltpu.VMEM),) * 2,
        scratch_shapes=[
            pltpu.VMEM((top_count, tok_rows), jnp.int32),
            pltpu.VMEM((top_count, tok_rows), F32),
            pltpu.VMEM(w_gate.shape, BF16),
            pltpu.VMEM(w_up.shape, BF16),
            pltpu.VMEM(w_down.shape, BF16),
            pltpu.VMEM((groups, *block), BF16),
            pltpu.VMEM((groups, *block), BF16),
            pltpu.VMEM((groups, table_rows, tok_rows), F32),
            pltpu.VMEM((groups, table_rows, tok_rows), F32),
            pltpu.VMEM((units, local_experts, lines, 2 * hid), BF16),
            pltpu.VMEM((units, local_experts, lines, 2 * hid), BF16),
            pltpu.VMEM((units, local_experts, lines, hid), BF16),
            pltpu.VMEM((units, local_experts, lines, hid), BF16),
            pltpu.VMEM((2, 2, local_experts, lines, width_part), BF16),
            pltpu.VMEM((2, CORES, *block), BF16),
            pltpu.VMEM((units, 2, *block), BF16),
            pltpu.VMEM((outer, 2, *block), BF16),
            pltpu.VMEM((outer, 2, *block), BF16),
            pltpu.VMEM((outer, 2, *block), BF16),
            pltpu.VMEM((outer, 2, *block), BF16),
            pltpu.VMEM((outer, 2, *block), BF16),
            dma((4,)), dma((3, local_experts)), dma((2,)),
            dma((groups,)), dma((groups,)),
            dma((outer, 2)), dma((outer, 2)),
            dma((outer, 2)), dma((outer, 2)),
            dma((outer, 2, 2)), dma((outer, 2, 2)),
            dma((units, 2, local_experts)), dma((units, 2, local_experts)),
            dma((units, 2)), dma((units, 2)),
            dma((outer, 2)), dma((outer, 2)),
            dma((outer, 2)), dma((outer, 2)),
        ],
        compiler_params=pltpu.CompilerParams(
            collective_id=0, has_side_effects=True, vmem_limit_bytes=60 * 1024 * 1024
        ),
    )(soft_tokens, out_grad, expert_ids.T, gate_mix.T, w_gate, w_up, w_down)
    return deliver(*parts)


def solution(mesh):
    in_specs = (
        P("expert", "dp"),
        P("expert", None),
        P("expert", None),
        P("expert", "dp", None),
        P("expert", "dp", None),
        P("expert", None, "dp"),
        P("expert", "dp"),
    )
    out_specs = (P("expert", "dp"), P("expert", "dp"))
    fits = mesh.shape["dp"] == 2 and mesh.shape["expert"] in (8, 16)
    return jax.shard_map(
        fused_device if fits else per_device,
        mesh=mesh, in_specs=in_specs, out_specs=out_specs, check_vma=False,
    )
```

```python
import functools

import jax
import jax.numpy as jnp
from jax import lax
from jax.experimental import pallas as pl
from jax.experimental.pallas import tpu as pltpu
from jax.sharding import PartitionSpec as P

F32 = jnp.float32
BF16 = jnp.bfloat16


def slot_maps(ids, mix, first, local_experts, capacity):
    tok_rows = ids.shape[1]
    own = first + jnp.arange(local_experts, dtype=jnp.int32)
    hit = ids[:, None, :, :] == own[None, :, None, None]
    named = jnp.any(hit, axis=3)
    weight = jnp.sum(jnp.where(hit, mix[:, None, :, :], 0.0), axis=3)
    before = jnp.arange(tok_rows)[:, None] < jnp.arange(tok_rows)[None, :]
    place = jnp.einsum(
        "set,tu->seu", named.astype(BF16), before.astype(BF16), preferred_element_type=F32
    ).astype(jnp.int32)
    slots = jnp.arange(capacity, dtype=jnp.int32)
    pick = (place[:, :, None, :] == slots[None, None, :, None]) & named[:, :, None, :]
    slot_weight = jnp.sum(jnp.where(pick, weight[:, :, None, :], 0.0), axis=3)
    return pick.astype(BF16), slot_weight


def per_device(soft_tokens, expert_ids, gate_mix, w_gate, w_up, w_down, out_grad):
    tok_rows, width_part = soft_tokens.shape
    top_count = expert_ids.shape[1]
    local_experts = w_gate.shape[0]
    hidden = w_gate.shape[2]
    groups = lax.axis_size("expert")
    dp_count = lax.axis_size("dp")
    experts = groups * local_experts
    capacity = max(2, tok_rows * top_count * 5 // (4 * experts))
    both = lax.all_gather(jnp.concatenate([soft_tokens, out_grad], axis=1), "expert")
    ids = lax.all_gather(expert_ids, "expert")
    mix = lax.all_gather(gate_mix, "expert")
    first = lax.axis_index("expert") * local_experts
    pick, slot_weight = slot_maps(ids, mix, first, local_experts, capacity)
    rows = jnp.einsum("sect,std->secd", pick, both, preferred_element_type=F32).astype(BF16)
    pre = [
        jnp.einsum("secd,edf->secf", rows[..., :width_part], w, preferred_element_type=F32)
        for w in (w_gate, w_up)
    ]
    back = jnp.einsum("secd,efd->secf", rows[..., width_part:], w_down, preferred_element_type=F32)
    part = jnp.concatenate(pre + [back], axis=-1).astype(BF16)
    total = part.astype(F32)
    moved = part
    for _ in range(dp_count - 1):
        moved = lax.ppermute(moved, "dp", [(i, (i + 1) % dp_count) for i in range(dp_count)])
        total = total + moved.astype(F32)
    a = total[..., :hidden]
    b = total[..., hidden : 2 * hidden]
    back = total[..., 2 * hidden :] * slot_weight[..., None]
    sig = jax.nn.sigmoid(a)
    act = (a * sig * b * slot_weight[..., None]).astype(BF16)
    d_gate = (back * b * sig * (1.0 + a * (1.0 - sig))).astype(BF16)
    d_up = (back * a * sig).astype(BF16)
    out = jnp.einsum("secf,efd->secd", act, w_down, preferred_element_type=F32)
    grad = jnp.einsum("secf,edf->secd", d_gate, w_gate, preferred_element_type=F32) + jnp.einsum(
        "secf,edf->secd", d_up, w_up, preferred_element_type=F32
    )
    result = jnp.concatenate([out, grad], axis=-1).astype(BF16)
    spread = jnp.einsum("sect,secd->std", pick, result, preferred_element_type=F32).astype(BF16)
    summed = lax.psum_scatter(spread, "expert", scatter_dimension=0, tiled=False)
    return summed[:, :width_part], summed[:, width_part:]


MESH = pl.DeviceIdType.MESH
MID = 2
CORES = 2
AHEAD = 4


def same(a, b):
    gap = (a - b) * (a - b)
    return 1 - lax.div(2 * gap, gap + 1)


def flip(value, step, count):
    out, bit = 0, 1
    while bit < count:
        out = out + lax.rem(lax.div(value, bit) + lax.div(step, bit), 2) * bit
        bit *= 2
    return out


def fused_kernel(
    groups, slots, tok_hbm, cot_hbm, ids_hbm, mix_hbm, wg_hbm, wu_hbm, wd_hbm, mixed_hbm, tgrad_hbm,
    ids_ref, mix_ref, wg_ref, wu_ref, wd_ref, ag_tok, ag_cot, table, metas,
    ysend_pre, yrecv_pre, ysend_back, yrecv_back, ready, acc, crecv, hold, xsend, xrecv, zsend, zrecv,
    lsem, wsem, osem, ms, mr, zs, zr, xs, xr, cs, cr, ys, yr, rcs, rcr, rxs, rxr, rzs, rzr,
):
    rows, half = tok_hbm.shape
    experts, _, hid = wg_ref.shape
    plane = MID * CORES
    outer = groups // plane
    units = 2 * outer
    me = lax.axis_index("expert")
    y = lax.axis_index("dp")
    z = lax.div(me, plane)
    x = lax.rem(lax.div(me, CORES), MID)
    c = lax.rem(me, CORES)
    core_peer = (z * MID + x) * CORES + 1 - c
    x_peer = (z * MID + 1 - x) * CORES + c
    other_dp = {"dp": 1 - y, "expert": me}
    ag = (ag_tok, ag_cot)
    outputs = (mixed_hbm, tgrad_hbm)
    ysend, yrecv = (ysend_pre, ysend_back), (yrecv_pre, yrecv_back)

    def at(expert):
        return {"dp": y, "expert": expert}

    def copy(src, dst, send, recv, device):
        return pltpu.make_async_remote_copy(
            src_ref=src, dst_ref=dst, send_sem=send, recv_sem=recv,
            device_id=device, device_id_type=MESH,
        )

    barrier = pltpu.get_barrier_semaphore()
    for k in range(1, groups):
        pl.semaphore_signal(
            barrier, inc=1, device_id=at(lax.rem(me + k, groups)), device_id_type=MESH
        )
    pl.semaphore_signal(barrier, inc=1, device_id=other_dp, device_id_type=MESH)

    loads = [
        pltpu.make_async_copy(src, dst, lsem.at[k])
        for k, (src, dst) in enumerate(
            ((ids_hbm, ids_ref), (mix_hbm, mix_ref), (tok_hbm, ag_tok.at[me]), (cot_hbm, ag_cot.at[me]))
        )
    ]

    def weight(which, e):
        src, dst = ((wg_hbm, wg_ref), (wu_hbm, wu_ref), (wd_hbm, wd_ref))[which]
        return pltpu.make_async_copy(src.at[e], dst.at[e], wsem.at[which, e])

    for load in loads:
        load.start()
    for e in range(experts):
        for which in range(3):
            weight(which, e).start()

    def dot(a, b, dims):
        return lax.dot_general(a, b, (dims, ((), ())), preferred_element_type=F32)

    def make_table():
        total = groups * experts
        expert = lax.broadcasted_iota(jnp.int32, (total, rows), 0)
        named = jnp.zeros((total, rows), F32)
        weight = jnp.zeros((total, rows), F32)
        for k in range(ids_ref.shape[0]):
            hit = expert == ids_ref[k : k + 1, :]
            named = named + jnp.where(hit, 1.0, 0.0)
            weight = weight + jnp.where(hit, mix_ref[k : k + 1, :], 0.0)
        before = lax.broadcasted_iota(jnp.int32, (rows, rows), 0) < lax.broadcasted_iota(
            jnp.int32, (rows, rows), 1
        )
        before = jnp.where(before, 1.0, 0.0).astype(BF16)
        place = dot(named.astype(BF16), before, ((1,), (0,)))
        key = jnp.where(named > 0.0, place, -4.0 * slots)
        table[...] = jnp.zeros_like(table)
        for d in range(groups):
            span = slice(d * experts, (d + 1) * experts)
            table[d, :experts, :] = key[span]
            table[d, experts : 2 * experts, :] = weight[span]

    loads[0].wait()
    loads[1].wait()
    make_table()
    metas[me] = table[me]
    loads[2].wait()
    loads[3].wait()
    pl.semaphore_wait(barrier, groups)

    def meta_copy(to):
        return copy(table.at[to], metas.at[me], ms.at[to], mr.at[me], at(to))

    def meta_arrival(source):
        return copy(table.at[source], metas.at[source], ms.at[source], mr.at[source], at(source))

    def peer_of(step):
        return (flip(z, step, outer) * MID + x) * CORES + c

    def z_copy(step, part):
        return copy(ag[part].at[me], ag[part].at[me], zs.at[step, part], zr.at[step, part], at(peer_of(step)))

    def z_arrival(step, part):
        blk = peer_of(step)
        return copy(ag[part].at[blk], ag[part].at[blk], zs.at[step, part], zr.at[step, part], at(blk))

    def x_copy(step, part, blk):
        return copy(
            ag[part].at[blk], ag[part].at[blk], xs.at[step, part], xr.at[step, part], at(x_peer)
        )

    def c_copy(step, across, part, blk):
        return copy(
            ag[part].at[blk], ag[part].at[blk],
            cs.at[step, across, part], cr.at[step, across, part], at(core_peer),
        )

    spans = (((0, hid), (hid, 2 * hid)), ((0, hid),))

    def y_copy(u, part, e, piece):
        low, high = spans[part][piece]
        here = (u, e, slice(None), slice(low, high))
        return copy(
            ysend[part].at[here], yrecv[part].at[here],
            ys.at[u, part, e, piece], yr.at[u, part, e, piece], other_dp,
        )

    def rc_copy(u, part):
        return copy(
            acc.at[part, 1 - c], crecv.at[u, part], rcs.at[u, part], rcr.at[u, part], at(core_peer)
        )

    def rx_copy(step, part):
        return copy(
            xsend.at[step, part], xrecv.at[step, part],
            rxs.at[step, part], rxr.at[step, part], at(x_peer),
        )

    def rz_copy(step, part):
        return copy(
            zsend.at[step, part], zrecv.at[step, part],
            rzs.at[step, part], rzr.at[step, part], at(peer_of(step)),
        )

    def step_of(u):
        g = lax.rem(lax.div(u + 1, 2), outer)
        return (lax.rem(g, outer - 1) + 1) * lax.div(g + outer - 1, outer)

    def across_of(u):
        first = 1 - lax.div(u + units - 1, units)
        last = lax.div(u + 1, units)
        swap = lax.div(u + 3, units) - lax.div(u + 1, units)
        flat = lax.rem(u + 1, 2)
        return flat + swap * (1 - 2 * flat) + last - first

    def base_of(u):
        across = across_of(u)
        return (flip(z, step_of(u), outer) * MID + x + across - 2 * x * across) * CORES

    order = [step for step in range(2, outer)] + [1]

    for part in range(2):
        c_copy(0, 0, part, me).start()
    meta_copy(core_peer).start()
    @pl.loop(1, groups)
    def _(k):
        to = lax.rem(me + k, groups)

        @pl.when(to != core_peer)
        def _():
            meta_copy(to).start()

    for part in range(2):
        z_copy(order[0], part).start()
    for part in range(2):
        x_copy(0, part, me).start()

    for part in range(2):
        for step in order[-1:] if outer > 2 else []:
            z_copy(step, part).start()

    def pick_of(u):
        base = base_of(u)
        tiles = metas[pl.ds(base, CORES)]
        slot = lax.broadcasted_iota(jnp.int32, (CORES * slots, CORES * rows), 0).astype(F32)
        picks, weights = [], []
        for e in range(experts):
            line = jnp.concatenate(
                [tiles[b, e : e + 1] + float(b * slots) for b in range(CORES)], axis=1
            )
            share = jnp.concatenate(
                [tiles[b, experts + e : experts + e + 1] for b in range(CORES)], axis=1
            )
            match = slot == line
            picks.append(jnp.where(match, 1.0, 0.0))
            weights.append(jnp.sum(jnp.where(match, share, 0.0), axis=1, keepdims=True))
        return jnp.concatenate(picks, axis=0), weights

    lines = CORES * slots

    def hand_on(step, part, col):
        z_arrival(step, part).wait_recv()
        x_copy(step, part, col).start()
        c_copy(step, 0, part, col).start()

    def first_half(i, u, part):
        step, across, base = step_of(u), across_of(u), base_of(u)
        col = base + c

        def arrive():
            @pl.when(across > 0)
            def _():
                x_copy(step, part, col).wait_recv()
                c_copy(step, 1, part, col).start()

            @pl.when(((1 - across) * step > 0) & (u != units - 2))
            def _():
                hand_on(step, part, col)

            c_copy(step, across, part, base + 1 - c).wait_recv()

        @pl.when(i < 2 * units)
        def _():
            arrive()

            if part == 0:
                for b in range(CORES):
                    @pl.when(base + b != me)
                    def _():
                        meta_arrival(base + b).wait_recv()

        @pl.when(i == 0)
        def _():
            weight(0, 0).wait()

        @pl.when(i == 1)
        def _():
            weight(2, 0).wait()

        @pl.when(i == 2)
        def _():
            for e in range(1, experts):
                for which in range(3):
                    weight(which, e).wait()

        pick, _ = pick_of(u)
        block = ag[part][pl.ds(base, CORES)].reshape(CORES * rows, half)
        got = dot(pick.astype(BF16), block, ((1,), (0,))).astype(BF16)
        for e in range(experts):
            @pl.when((i < 2 * units) if e == 0 else (i >= 2))
            def _():
                mine = got[e * lines : (e + 1) * lines]
                if part == 0:
                    for piece, w_ref in enumerate((wg_ref, wu_ref)):
                        low, high = spans[0][piece]
                        if piece == 1 and e == 0:
                            @pl.when(i == 0)
                            def _():
                                weight(1, 0).wait()

                        value = dot(mine, w_ref[e], ((1,), (0,)))
                        ysend_pre[u, e, :, low:high] = value.astype(BF16)
                        y_copy(u, 0, e, piece).start()
                else:
                    ysend_back[u, e] = dot(mine, wd_ref[e], ((1,), (1,))).astype(BF16)
                    y_copy(u, 1, e, 0).start()

    def sums(u, e):
        def total(lo):
            piece = ysend_pre[u, e, :, lo : lo + hid].astype(F32)
            return piece + yrecv_pre[u, e, :, lo : lo + hid].astype(F32)

        return total(0), total(hid)

    def mixed_half(u, e, share):
        for piece in range(2):
            y_copy(u, 0, e, piece).wait_recv()
        a, b = sums(u, e)
        act = (a * jax.nn.sigmoid(a) * b * share).astype(BF16)
        return dot(act, wd_ref[e], ((1,), (0,))).astype(BF16)

    def grad_half(u, e, share):
        a, b = sums(u, e)
        sig = jax.nn.sigmoid(a)
        by_gate = b * sig * (1.0 + a * (1.0 - sig))
        by_up = a * sig
        y_copy(u, 1, e, 0).wait_recv()
        back = (ysend_back[u, e].astype(F32) + yrecv_back[u, e].astype(F32)) * share
        d_gate = (back * by_gate).astype(BF16)
        d_up = (back * by_up).astype(BF16)
        grad = dot(d_gate, wg_ref[e], ((1,), (1,))) + dot(d_up, wu_ref[e], ((1,), (1,)))
        return grad.astype(BF16)

    def to_x_peer(u, part):
        step, across = step_of(u), across_of(u)
        rc_copy(u, part).wait_recv()
        both = (acc[part, c].astype(F32) + crecv[u, part].astype(F32)).astype(BF16)

        @pl.when(across == 0)
        def _():
            hold[step, part] = both

        @pl.when(across > 0)
        def _():
            xsend[step, part] = both
            rx_copy(step, part).start()

        rc_copy(u, part).wait_send()

    def to_owner(step, part):
        rx_copy(step, part).wait_recv()
        here = hold[step, part].astype(F32) + xrecv[step, part].astype(F32)
        zsend[step, part] = here.astype(BF16)
        rz_copy(step, part).start()

    def item(i):
        pair = lax.div(i, 2)
        moved = (units - 1) * (same(pair, 1) - same(pair, units))
        u, part = pair - 1 + same(pair, 0) + moved, lax.rem(i, 2)
        return u, part

    def second_half(i, u, part):
        step, before = step_of(u), step_of(u - 1 + lax.div(units - u, units))
        kept = lax.div(units - u, units)

        @pl.when((u > 1) & (u < units - 1) & (lax.rem(u, 2) == 1))
        def _():
            to_owner(before, part)

        pick, shares = pick_of(u)
        spread_by = pick.T.astype(BF16)
        for e in range(experts):
            @pl.when((i < 2 * units) if e == 0 else (i >= 2))
            def _():
                ready[kept, part, e] = (grad_half if part else mixed_half)(u, e, shares[e])

        @pl.when(i >= 2)
        def _():
            values = ready[kept, part].reshape(experts * lines, half)
            spread = dot(spread_by, values, ((1,), (0,)))
            acc[part] = spread.astype(BF16).reshape(CORES, rows, half)
            rc_copy(u, part).start()

        @pl.when((i >= 2) & (i < 2 * units))
        def _():
            to_x_peer(u, part)

        @pl.when(u == units - 2)
        def _():
            to_owner(step, part)

    def out_copy(part):
        return pltpu.make_async_copy(zsend.at[0, part], outputs[part], osem.at[part])

    def finish(part):
        for step in order:
            rz_copy(step, part).wait_recv()
        rx_copy(0, part).wait_recv()
        final = xrecv[0, part].astype(F32)
        for step in order:
            final = final + zrecv[step, part].astype(F32)
        rc_copy(0, part).wait_recv()
        final = final + acc[part, c].astype(F32) + crecv[0, part].astype(F32)
        outputs[part][...] = final.astype(BF16)

    @pl.loop(0, 2 * units + 2 + AHEAD)
    def _(i):
        @pl.when(i < 2 * units + 2)
        def _():
            u, part = item(i)
            for which in range(2):
                @pl.when(part == which)
                def _():
                    first_half(i, u, which)

            @pl.when(i == 2 * outer - 1)
            def _():
                for which in range(2):
                    hand_on(order[-1], which, peer_of(order[-1]))

            for later, step in enumerate(order[1:-1]):
                @pl.when(i == 4 * later + 5)
                def _():
                    for which in range(2):
                        z_copy(step, which).start()

        @pl.when(i >= AHEAD)
        def _():
            u, part = item(i - AHEAD)
            for which in range(2):
                @pl.when(part == which)
                def _():
                    second_half(i - AHEAD, u, which)

    finish(0)
    finish(1)

    @pl.loop(1, groups)
    def _(k):
        meta_copy(lax.rem(me + k, groups)).wait_send()

    for part in range(2):
        for step in range(outer):
            x_copy(step, part, me).wait_send()
            rx_copy(step, part).wait_send()
            for across in range(2):
                c_copy(step, across, part, me).wait_send()
            if step:
                z_copy(step, part).wait_send()
                rz_copy(step, part).wait_send()
        for u in range(units):
            for e in range(experts):
                for piece in range(len(spans[part])):
                    y_copy(u, part, e, piece).wait_send()
        rc_copy(0, part).wait_send()


def deliver(*parts):
    def move(a_ref, b_ref, c_ref, d_ref, sem):
        copies = [
            pltpu.make_async_copy(src, dst, sem.at[k])
            for k, (src, dst) in enumerate(((a_ref, c_ref), (b_ref, d_ref)))
        ]
        for one in copies:
            one.start()
        for one in copies:
            one.wait()

    return pl.pallas_call(
        move, out_shape=tuple(jax.ShapeDtypeStruct(p.shape, p.dtype) for p in parts),
        in_specs=[pl.BlockSpec(memory_space=pltpu.VMEM)] * 2,
        out_specs=(pl.BlockSpec(memory_space=pl.ANY),) * 2,
        scratch_shapes=[pltpu.SemaphoreType.DMA((2,))],
    )(*(pltpu.with_memory_space_constraint(p, pltpu.VMEM) for p in parts))


def fused_device(soft_tokens, expert_ids, gate_mix, w_gate, w_up, w_down, out_grad):
    tok_rows, width_part = soft_tokens.shape
    top_count = expert_ids.shape[1]
    local_experts, _, hid = w_gate.shape
    groups = lax.axis_size("expert")
    experts = groups * local_experts
    capacity = max(2, tok_rows * top_count * 5 // (4 * experts))
    plane = MID * CORES
    outer = groups // plane
    units = 2 * outer
    lines = CORES * capacity
    hbm = pl.BlockSpec(memory_space=pl.ANY)
    dma = pltpu.SemaphoreType.DMA
    out = pltpu.VMEM((tok_rows, width_part), BF16)
    table_rows = -(-2 * local_experts // 8) * 8
    block = (tok_rows, width_part)
    parts = pl.pallas_call(
        functools.partial(fused_kernel, groups, capacity),
        out_shape=(out, out),
        in_specs=[hbm] * 7,
        out_specs=(pl.BlockSpec(memory_space=pltpu.VMEM),) * 2,
        scratch_shapes=[
            pltpu.VMEM((top_count, tok_rows), jnp.int32),
            pltpu.VMEM((top_count, tok_rows), F32),
            pltpu.VMEM(w_gate.shape, BF16),
            pltpu.VMEM(w_up.shape, BF16),
            pltpu.VMEM(w_down.shape, BF16),
            pltpu.VMEM((groups, *block), BF16),
            pltpu.VMEM((groups, *block), BF16),
            pltpu.VMEM((groups, table_rows, tok_rows), F32),
            pltpu.VMEM((groups, table_rows, tok_rows), F32),
            pltpu.VMEM((units, local_experts, lines, 2 * hid), BF16),
            pltpu.VMEM((units, local_experts, lines, 2 * hid), BF16),
            pltpu.VMEM((units, local_experts, lines, hid), BF16),
            pltpu.VMEM((units, local_experts, lines, hid), BF16),
            pltpu.VMEM((2, 2, local_experts, lines, width_part), BF16),
            pltpu.VMEM((2, CORES, *block), BF16),
            pltpu.VMEM((units, 2, *block), BF16),
            pltpu.VMEM((outer, 2, *block), BF16),
            pltpu.VMEM((outer, 2, *block), BF16),
            pltpu.VMEM((outer, 2, *block), BF16),
            pltpu.VMEM((outer, 2, *block), BF16),
            pltpu.VMEM((outer, 2, *block), BF16),
            dma((4,)), dma((3, local_experts)), dma((2,)),
            dma((groups,)), dma((groups,)),
            dma((outer, 2)), dma((outer, 2)),
            dma((outer, 2)), dma((outer, 2)),
            dma((outer, 2, 2)), dma((outer, 2, 2)),
            dma((units, 2, local_experts, 2)), dma((units, 2, local_experts, 2)),
            dma((units, 2)), dma((units, 2)),
            dma((outer, 2)), dma((outer, 2)),
            dma((outer, 2)), dma((outer, 2)),
        ],
        compiler_params=pltpu.CompilerParams(
            collective_id=0, has_side_effects=True, vmem_limit_bytes=60 * 1024 * 1024
        ),
    )(soft_tokens, out_grad, expert_ids.T, gate_mix.T, w_gate, w_up, w_down)
    return deliver(*parts)


def solution(mesh):
    in_specs = (
        P("expert", "dp"),
        P("expert", None),
        P("expert", None),
        P("expert", "dp", None),
        P("expert", "dp", None),
        P("expert", None, "dp"),
        P("expert", "dp"),
    )
    out_specs = (P("expert", "dp"), P("expert", "dp"))
    fits = mesh.shape["dp"] == 2 and mesh.shape["expert"] in (8, 16)
    return jax.shard_map(
        fused_device if fits else per_device,
        mesh=mesh, in_specs=in_specs, out_specs=out_specs, check_vma=False,
    )
```
